32 devices in a mesh: dp: 8 (over y, x, core), ctx: 4 (over z).
Axes of the slice: x: 2, y: 2, z: 4, core: 2. Of those that a mesh axis runs over, the one named last changes fastest.
Arguments:
- tokens: bfloat16 [8, 2048, 960], P('dp', 'ctx'), may hold values from -6 to 6
- cotangent: bfloat16 [8, 2048, 960], P('dp', 'ctx'), may hold values from -6 to 6
- lengths: int32 [8], P('dp'), may hold values from 512 to 2048, as said below
- gate_mask: int32 [8, 2048], P('dp', 'ctx'), may hold values 0 or 1
- block_order: int32 [8], replicated, may hold values from 0 to 7, as said below
- w_query: bfloat16 [921600], P(('dp', 'ctx')), may hold values from -0.1875 to 0.1875
- w_key: bfloat16 [307200], P(('dp', 'ctx')), may hold values from -0.1875 to 0.1875
- w_value: bfloat16 [307200], P(('dp', 'ctx')), may hold values from -0.1875 to 0.1875
- w_out: bfloat16 [921600], P(('dp', 'ctx')), may hold values from -1.5 to 1.5
- w_gate: bfloat16 [2457600], P(('dp', 'ctx')), may hold values from -0.1875 to 0.1875
- w_up: bfloat16 [2457600], P(('dp', 'ctx')), may hold values from -0.1875 to 0.1875
- w_down: bfloat16 [2457600], P(('dp', 'ctx')), may hold values from -0.125 to 0.125
- gain_attn: float32 [960], replicated, may hold values from 0.5 to 1.5
- gain_mlp: float32 [960], replicated, may hold values from 0.5 to 1.5
- w_router: float32 [960], replicated, may hold values from -0.1875 to 0.1875
Outputs:
- out_tokens: bfloat16 [8, 2048, 960], P('dp', 'ctx')
- grad_tokens: bfloat16 [8, 2048, 960], P('dp', 'ctx')
- grad_query: float32 [921600], P(('dp', 'ctx'))
- grad_key: float32 [307200], P(('dp', 'ctx'))
- grad_value: float32 [307200], P(('dp', 'ctx'))
- grad_out: float32 [921600], P(('dp', 'ctx'))
- grad_gate: float32 [2457600], P(('dp', 'ctx'))
- grad_up: float32 [2457600], P(('dp', 'ctx'))
- grad_down: float32 [2457600], P(('dp', 'ctx'))
- grad_gain_attn: float32 [960], replicated
- grad_gain_mlp: float32 [960], replicated
- grad_router: float32 [960], replicated
The draws below stay inside these ranges and needn't reach their ends.
Inputs may be any that keep to these rules, and one draw needn't show every extreme that they name: `lengths`: every sequence has between 512 and 2048 valid tokens; some sequence has exactly 2048 and some exactly 512. `block_order`: stored blocks 2 c and 2 c + 1 hold causal blocks k and 7 - k, in either order; every causal block appears once.
All inputs are finite; a program needn't handle non-finite values. No bound on the sum of `gate_mask` on one device may be relied on, other than what follows from the above.
Results may differ from the reference program's by a relative error of at most 0.014.
Values may be sent and summed in bfloat16 or wider, within the bound.
No kernel may reach another device: no remote copies, remote signals or barrier semaphores. Data moves between devices by JAX's collectives and lax.ppermute only.
A program may use at most 192 MiB of HBM per device.

```python
import jax
import jax.numpy as jnp
from jax import lax

D = 960
HEADS = 15
KV_HEADS = 5
HEAD_DIM = 64
FF = 2560
KV_WIDTH = 320
SEQ_LEN = 2048
BLOCK = 256
BLOCKS = 8
SEQS = 8
MIN_LEN = 512


def draw_lengths(key, part):
    drawn_len = jax.random.randint(key, (SEQS,), MIN_LEN, SEQ_LEN + 1, dtype=jnp.int32)
    picked = jax.random.permutation(jax.random.fold_in(key, 7), SEQS)
    drawn_len = drawn_len.at[picked[0]].set(SEQ_LEN)
    return drawn_len.at[picked[1]].set(MIN_LEN).astype(jnp.int32)


def draw_block_order(key, part):
    half_count = BLOCKS // 2
    low_blocks = jax.random.permutation(key, half_count).astype(jnp.int32)
    high_blocks = (BLOCKS - 1 - low_blocks).astype(jnp.int32)
    coin_flips = jax.random.randint(jax.random.fold_in(key, 3), (half_count,), 0, 2, dtype=jnp.int32)
    first_col = jnp.where(coin_flips == 1, high_blocks, low_blocks)
    second_col = low_blocks + high_blocks - first_col
    return jnp.stack([first_col, second_col], axis=1).reshape(-1).astype(jnp.int32)


def touch_ends(drawn, key, smallest, high):
    longest = drawn.shape.index(max(drawn.shape))
    spots = []
    for shift in (0, 1):
        where = [jax.random.randint(jax.random.fold_in(key, axis), (), 0, length) for axis, length in enumerate(drawn.shape)]
        where[longest] = (where[longest] + shift) % drawn.shape[longest]
        spots.append(tuple(where))
    return drawn.at[spots[0]].set(smallest).at[spots[1]].set(high)


def block_levels(stream_key, extent, cuts, smallest, top_value):
    gain, own = 1.0, jax.random.fold_in(stream_key, 6)
    for position, parts in cuts:
        heights = jnp.exp(jax.random.uniform(jax.random.fold_in(own, position), (parts,), jnp.float32, smallest / len(cuts), top_value / len(cuts)))
        gain = gain * jnp.repeat(heights, extent[position] // parts).reshape([-1 if axis == position else 1 for axis in range(len(extent))])
    return gain


def noise(stream_key, dims, deviation, reach, pieces=(), kind=jnp.bfloat16):
    factor_of = block_levels(stream_key, dims, pieces, -0.22, 0.18) if pieces else 1.0
    array = jax.random.normal(stream_key, dims, jnp.float32) * deviation * factor_of
    return jnp.minimum(jnp.maximum(array, -reach), reach).astype(kind)


def setup_inputs(seed: int = 0) -> dict:
    key_of = jax.random.split(jax.random.key(seed), 16)
    return {
        "tokens": noise(key_of[0], (SEQS, SEQ_LEN, D), 1.0, 6.0, ((0, 8), (1, 4))),
        "cotangent": noise(key_of[1], (SEQS, SEQ_LEN, D), 1.0, 6.0, ((0, 8), (1, 4))),
        "lengths": draw_lengths(jax.random.fold_in(key_of[15], 71), 0),
        "gate_mask": touch_ends((jax.random.randint(key_of[3], (SEQS, SEQ_LEN), 0, 3) < 2).astype(jnp.int32), jax.random.fold_in(key_of[3], 1), 0, 1),
        "block_order": draw_block_order(jax.random.fold_in(key_of[15], 71), 0),
        "w_query": noise(key_of[5], (D * D,), D ** -0.5, 0.1875, ((0, 32),)),
        "w_key": noise(key_of[6], (D * KV_WIDTH,), D ** -0.5, 0.1875, ((0, 32),)),
        "w_value": noise(key_of[7], (D * KV_WIDTH,), D ** -0.5, 0.1875, ((0, 32),)),
        "w_out": noise(key_of[8], (D * D,), 16 ** -0.5, 1.5, ((0, 32),)),
        "w_gate": noise(key_of[9], (D * FF,), D ** -0.5, 0.1875, ((0, 32),)),
        "w_up": noise(key_of[10], (D * FF,), D ** -0.5, 0.1875, ((0, 32),)),
        "w_down": noise(key_of[11], (FF * D,), FF ** -0.5, 0.125, ((0, 32),)),
        "gain_attn": jnp.clip(1.0 + 0.1 * jax.random.normal(key_of[12], (D,), jnp.float32), 0.5, 1.5),
        "gain_mlp": jnp.clip(1.0 + 0.1 * jax.random.normal(key_of[13], (D,), jnp.float32), 0.5, 1.5),
        "w_router": noise(key_of[14], (D,), D ** -0.5, 0.1875, (), jnp.float32),
    }


@jax.custom_vjp
def low(v):
    return lax.optimization_barrier(v.astype(jnp.bfloat16)).astype(jnp.float32)

@jax.custom_vjp
def low_back(v):
    return v

def low_keep(v):
    return (low(v), None)

def low_pass(kept, grad):
    return (grad,)

def back_keep(v):
    return (v, None)

def back_low(kept, grad):
    return (low(grad),)
low.defvjp(low_keep, low_pass)
low_back.defvjp(back_keep, back_low)
norm_eps = 1e-05
rope_base = 100000.0
neg_big = -1e+30
highest = lax.Precision.HIGHEST

def product(left, right):
    return jnp.dot(left, right, precision=highest)

def rms_norm(values_in, gain_vec):
    return values_in * lax.rsqrt(lax.optimization_barrier(jnp.mean(values_in * values_in, axis=-1, keepdims=True)) + norm_eps) * gain_vec

def rotary(positions, head_width):
    frequency = rope_base ** (-jnp.arange(0, head_width, 2).astype(jnp.float32) / head_width)
    angles = positions.astype(jnp.float32)[:, None] * frequency[None, :]
    return (jnp.cos(angles)[:, None, :], jnp.sin(angles)[:, None, :])

def rotate(tensor, cosine, sine_table):
    half_width = tensor.shape[-1] // 2
    first_half = tensor[..., :half_width]
    second = tensor[..., half_width:]
    return jnp.concatenate([first_half * cosine - second * sine_table, second * cosine + first_half * sine_table], axis=-1)

def attend(queries, key_heads, value_heads, positions, length):
    row_count = queries.shape[0]
    block_rows = min(512, row_count)
    kv_count = key_heads.shape[1]
    group_size = queries.shape[1] // kv_count
    head_width = queries.shape[2]
    blocks = queries.reshape(row_count // block_rows, block_rows, kv_count, group_size, head_width)
    block_pos = positions.reshape(row_count // block_rows, block_rows)
    usable = positions < length
    score_scale = head_width ** (-0.5)

    def one_block(packed):
        block_q, query_pos = packed
        raw_scores = jnp.einsum('qhgd,khd->hgqk', block_q, key_heads, precision=highest) * score_scale
        scores = low_back(raw_scores)
        allowed = (positions[None, :] <= query_pos[:, None]) & usable[None, :]
        weights = low(jax.nn.softmax(jnp.where(allowed[None, None], scores, neg_big), axis=-1))
        return jnp.einsum('hgqk,khd->qhgd', weights, value_heads, precision=highest)
    result = lax.map(jax.checkpoint(one_block), (blocks, block_pos))
    return result.reshape(row_count, kv_count * group_size, head_width)

def forward(inputs, params, positions, length, gate_bits):
    weight_query, weight_key, weight_value, weight_out, weight_gate, weight_up, weight_down, gain_attn, gain_mlp, w_router = params
    row_count = inputs.shape[0]
    cosine, sine_table = rotary(positions, HEAD_DIM)
    normed = low(rms_norm(inputs, gain_attn))
    queries = low(rotate(low_back(product(normed, weight_query)).reshape(row_count, HEADS, HEAD_DIM), cosine, sine_table))
    key_heads = low(rotate(low_back(product(normed, weight_key)).reshape(row_count, KV_HEADS, HEAD_DIM), cosine, sine_table))
    value_heads = low(low_back(product(normed, weight_value))).reshape(row_count, KV_HEADS, HEAD_DIM)
    mixed = low(low_back(attend(queries, key_heads, value_heads, positions, length))).reshape(row_count, D)
    attn_out = low_back(product(mixed, weight_out))
    middle = inputs + attn_out
    normed_mlp = low(rms_norm(middle, gain_mlp))
    gate_proj = low_back(product(normed_mlp, weight_gate))
    up_proj = low_back(product(normed_mlp, weight_up))
    hidden = low(jax.nn.silu(gate_proj) * up_proj)
    mlp_out = low_back(product(hidden, weight_down))
    chosen = gate_bits * jax.nn.sigmoid(product(inputs, w_router))
    return inputs + chosen[:, None] * (attn_out + mlp_out)

def reference(tokens, cotangent, lengths, gate_mask, block_order, w_query, w_key, w_value, w_out, w_gate, w_up, w_down, gain_attn, gain_mlp, w_router):
    matrices = (w_query.astype(jnp.float32).reshape(D, D), w_key.astype(jnp.float32).reshape(D, KV_WIDTH), w_value.astype(jnp.float32).reshape(D, KV_WIDTH), w_out.astype(jnp.float32).reshape(D, D), w_gate.astype(jnp.float32).reshape(D, FF), w_up.astype(jnp.float32).reshape(D, FF), w_down.astype(jnp.float32).reshape(FF, D))
    params = matrices + (gain_attn.astype(jnp.float32), gain_mlp.astype(jnp.float32), w_router.astype(jnp.float32))
    starts = jnp.arange(SEQ_LEN, dtype=jnp.int32)
    positions = (block_order[starts // BLOCK] * BLOCK + starts % BLOCK).astype(jnp.int32)

    def one_sequence(totals, element):
        seq_tokens, seq_cotangent, length, gate_row = element
        inputs = seq_tokens.astype(jnp.float32)
        usable = (positions < length).astype(jnp.float32)
        gate_bits = gate_row.astype(jnp.float32)

        def run_block(inputs_now, weights_now):
            return forward(inputs_now, weights_now, positions, length, gate_bits)
        result, pullback = jax.vjp(run_block, inputs, params)
        grad_x, grad_params = pullback(seq_cotangent.astype(jnp.float32) * usable[:, None])
        totals = jax.tree.map(lambda a, b: a + b, totals, grad_params)
        return (totals, (result.astype(jnp.bfloat16), grad_x.astype(jnp.bfloat16)))
    zero_totals = jax.tree.map(jnp.zeros_like, params)
    totals, (outputs, input_grads) = lax.scan(one_sequence, zero_totals, (tokens, cotangent, lengths, gate_mask))
    return (outputs, input_grads, totals[0].reshape(-1), totals[1].reshape(-1), totals[2].reshape(-1), totals[3].reshape(-1), totals[4].reshape(-1), totals[5].reshape(-1), totals[6].reshape(-1), totals[7], totals[8], totals[9])
```

```python
import functools

import jax
import jax.numpy as jnp
from jax import lax
from jax.experimental import pallas as pl
from jax.experimental.pallas import tpu as pltpu
from jax.sharding import PartitionSpec as P

HEADS = 15
KV_HEADS = 5
HEAD_DIM = 64
FF = 2560

norm_eps = 1e-05
rope_base = 100000.0
neg_big = -1e30
f32 = jnp.float32
bf16 = jnp.bfloat16

block_bits = (0, 2, 4, 6, 1, 3, 5, 7)


def dot_nn(left, right):
    return lax.dot_general(left, right, (((1,), (0,)), ((), ())), preferred_element_type=f32)


def dot_tn(left, right):
    return lax.dot_general(left, right, (((0,), (0,)), ((), ())), preferred_element_type=f32)


def dot_nt(left, right):
    return lax.dot_general(left, right, (((1,), (1,)), ((), ())), preferred_element_type=f32)


def attend_body(first, last, pieces, head_width, group_size, block, sc, *refs):
    q_ref = refs[0]
    kv_refs = refs[1 : 1 + pieces]
    at = 1 + pieces
    if not first:
        m_in, l_in, acc_in = refs[at : at + 3]
        at += 3
    if last:
        o_ref, lse_ref = refs[at : at + 2]
        at += 2
        m_ref, l_ref, acc_ref = refs[at : at + 3]
    else:
        m_out, l_out, acc_out = refs[at : at + 3]
        m_ref, l_ref, acc_ref = m_out.at[0], l_out.at[0], acc_out.at[0]
    length = sc[0]
    width = group_size * block
    for qb in range(2):
        q_blk = sc[1 + qb]
        cols = slice(qb * block, (qb + 1) * block)
        q_cat = jnp.concatenate(
            [q_ref[h * head_width : (h + 1) * head_width, cols] for h in range(group_size)], axis=1
        )
        if first:
            m_ref[qb : qb + 1, :] = jnp.full((1, width), neg_big, f32)
            l_ref[qb : qb + 1, :] = jnp.zeros((1, width), f32)
            acc_ref[qb] = jnp.zeros((head_width, width), f32)
        else:
            m_ref[qb : qb + 1, :] = m_in[0, qb : qb + 1, :]
            l_ref[qb : qb + 1, :] = l_in[0, qb : qb + 1, :]
            acc_ref[qb] = acc_in[0, qb]
        for piece in range(pieces):
            for sub in range(2):
                k_blk = sc[3 + 2 * piece + sub]
                start = k_blk * block
                keys = slice(sub * block, (sub + 1) * block)

                def step(masked, piece=piece, keys=keys, k_blk=k_blk, start=start):
                    key_t = kv_refs[piece][0, :, keys]
                    val_t = kv_refs[piece][1, :, keys]
                    scores = dot_tn(key_t, q_cat)
                    if masked:
                        k_pos = start + lax.broadcasted_iota(jnp.int32, (block, block), 0)
                        q_pos = q_blk * block + lax.broadcasted_iota(jnp.int32, (block, block), 1)
                        seen = (k_pos <= q_pos) & (k_pos < length)
                        scores = jnp.concatenate(
                            [
                                jnp.where(seen, scores[:, h * block : (h + 1) * block], neg_big)
                                for h in range(group_size)
                            ],
                            axis=1,
                        )
                    m_old = m_ref[qb : qb + 1, :]
                    m_new = jnp.maximum(m_old, jnp.max(scores, axis=0, keepdims=True))
                    probs = jnp.exp(scores - m_new)
                    alpha = jnp.exp(m_old - m_new)
                    m_ref[qb : qb + 1, :] = m_new
                    l_ref[qb : qb + 1, :] = alpha * l_ref[qb : qb + 1, :] + jnp.sum(
                        probs, axis=0, keepdims=True
                    )
                    acc_ref[qb] = acc_ref[qb] * alpha + dot_nn(val_t, probs.astype(bf16))

                live = (k_blk <= q_blk) & (start < length)
                plain = (k_blk < q_blk) & (start + block <= length)
                pl.when(plain)(functools.partial(step, False))
                pl.when(live & jnp.logical_not(plain))(functools.partial(step, True))
        if last:
            total = l_ref[qb : qb + 1, :]
            out = acc_ref[qb] * (1.0 / total)
            for h in range(group_size):
                o_ref[h * head_width : (h + 1) * head_width, cols] = out[
                    :, h * block : (h + 1) * block
                ].astype(bf16)
            lse_ref[0, qb : qb + 1, :] = m_ref[qb : qb + 1, :] + jnp.log(total)


def attend_call(scalars, q_t, pieces, state, last, group_size, head_width):
    rows, tokens = q_t.shape
    kv_count = rows // (group_size * head_width)
    block = tokens // 2
    width = group_size * block
    first = state is None
    q_spec = pl.BlockSpec((group_size * head_width, tokens), lambda g, sc: (g, 0))
    kv_spec = pl.BlockSpec((2, head_width, tokens), lambda g, sc: (0, g, 0))
    row_spec = pl.BlockSpec((1, 2, width), lambda g, sc: (g, 0, 0))
    acc_spec = pl.BlockSpec((1, 2, head_width, width), lambda g, sc: (g, 0, 0, 0))
    row_shape = jax.ShapeDtypeStruct((kv_count, 2, width), f32)
    acc_shape = jax.ShapeDtypeStruct((kv_count, 2, head_width, width), f32)
    in_specs = [q_spec] + [kv_spec] * len(pieces)
    operands = [q_t] + list(pieces)
    aliases = {}
    if not first:
        in_specs += [row_spec, row_spec, acc_spec]
        operands += list(state)
    if last:
        out_specs = [q_spec, row_spec]
        out_shape = [jax.ShapeDtypeStruct((rows, tokens), bf16), row_shape]
        scratch = [
            pltpu.VMEM((2, width), f32),
            pltpu.VMEM((2, width), f32),
            pltpu.VMEM((2, head_width, width), f32),
        ]
    else:
        out_specs = [row_spec, row_spec, acc_spec]
        out_shape = [row_shape, row_shape, acc_shape]
        scratch = []
    body = functools.partial(
        attend_body, first, last, len(pieces), head_width, group_size, block
    )
    work = kv_count * len(pieces) * tokens * tokens * group_size
    return pl.pallas_call(
        body,
        grid_spec=pltpu.PrefetchScalarGridSpec(
            num_scalar_prefetch=1,
            grid=(kv_count,),
            in_specs=in_specs,
            out_specs=out_specs,
            scratch_shapes=scratch,
        ),
        out_shape=out_shape,
        input_output_aliases=aliases,
        name="attend_forward",
        cost_estimate=pl.CostEstimate(
            flops=4 * work * head_width, transcendentals=work, bytes_accessed=4 * rows * tokens
        ),
    )(scalars, *operands)


def attend_back_body(first, pieces, head_width, group_size, block, sc, *refs):
    q_ref, do_ref, o_ref, lse_ref = refs[:4]
    kv_refs = refs[4 : 4 + pieces]
    at = 4 + pieces
    if not first:
        dq_in = refs[at]
        at += 1
    dq_ref = refs[at]
    dkv_refs = refs[at + 1 : at + 1 + pieces]
    dkv_acc = refs[at + 1 + pieces]
    length = sc[0]
    dkv_acc[...] = jnp.zeros(dkv_acc.shape, f32)
    if first:
        dq_ref[...] = jnp.zeros(dq_ref.shape, f32)
    else:
        dq_ref[...] = dq_in[...]
    for qb in range(2):
        q_blk = sc[1 + qb]
        cols = slice(qb * block, (qb + 1) * block)

        def side_by_side(ref, cols=cols):
            return jnp.concatenate(
                [ref[h * head_width : (h + 1) * head_width, cols] for h in range(group_size)],
                axis=1,
            )

        q_cat = side_by_side(q_ref)
        do_cat = side_by_side(do_ref)
        o_cat = side_by_side(o_ref)
        delta = jnp.sum(do_cat.astype(f32) * o_cat.astype(f32), axis=0, keepdims=True)
        lse = lse_ref[0, qb : qb + 1, :]
        for piece in range(pieces):
            for sub in range(2):
                k_blk = sc[3 + 2 * piece + sub]
                start = k_blk * block
                keys = slice(sub * block, (sub + 1) * block)

                def step(
                    masked, piece=piece, keys=keys, start=start, q_blk=q_blk, q_cat=q_cat,
                    do_cat=do_cat, delta=delta, lse=lse, cols=cols,
                ):
                    key_t = kv_refs[piece][0, :, keys]
                    val_t = kv_refs[piece][1, :, keys]
                    scores = dot_tn(key_t, q_cat)
                    if masked:
                        k_pos = start + lax.broadcasted_iota(jnp.int32, (block, block), 0)
                        q_pos = q_blk * block + lax.broadcasted_iota(jnp.int32, (block, block), 1)
                        seen = (k_pos <= q_pos) & (k_pos < length)
                        scores = jnp.concatenate(
                            [
                                jnp.where(seen, scores[:, h * block : (h + 1) * block], neg_big)
                                for h in range(group_size)
                            ],
                            axis=1,
                        )
                    probs = jnp.exp(scores - lse)
                    d_probs = dot_tn(val_t, do_cat)
                    d_scores = (probs * (d_probs - delta)).astype(bf16)
                    dkv_acc[piece, 1, :, keys] += dot_nt(do_cat, probs.astype(bf16))
                    dkv_acc[piece, 0, :, keys] += dot_nt(q_cat, d_scores)
                    dq = dot_nn(key_t, d_scores)
                    for h in range(group_size):
                        dq_ref[h * head_width : (h + 1) * head_width, cols] += dq[
                            :, h * block : (h + 1) * block
                        ]

                live = (k_blk <= q_blk) & (start < length)
                plain = (k_blk < q_blk) & (start + block <= length)
                pl.when(plain)(functools.partial(step, False))
                pl.when(live & jnp.logical_not(plain))(functools.partial(step, True))
    for piece in range(pieces):
        dkv_refs[piece][...] = dkv_acc[piece].astype(dkv_refs[piece].dtype)


def attend_back_call(scalars, q_t, do_t, o_t, lse, pieces, dq_before, types, group_size, head_width):
    rows, tokens = q_t.shape
    kv_count = rows // (group_size * head_width)
    block = tokens // 2
    width = group_size * block
    first = dq_before is None
    q_spec = pl.BlockSpec((group_size * head_width, tokens), lambda g, sc: (g, 0))
    kv_spec = pl.BlockSpec((2, head_width, tokens), lambda g, sc: (0, g, 0))
    row_spec = pl.BlockSpec((1, 2, width), lambda g, sc: (g, 0, 0))
    in_specs = [q_spec, q_spec, q_spec, row_spec] + [kv_spec] * len(pieces)
    operands = [q_t, do_t, o_t, lse] + list(pieces)
    aliases = {}
    if not first:
        in_specs.append(q_spec)
        operands.append(dq_before)
        aliases = {len(operands): 0}
    body = functools.partial(attend_back_body, first, len(pieces), head_width, group_size, block)
    work = kv_count * len(pieces) * tokens * tokens * group_size
    return pl.pallas_call(
        body,
        grid_spec=pltpu.PrefetchScalarGridSpec(
            num_scalar_prefetch=1,
            grid=(kv_count,),
            in_specs=in_specs,
            out_specs=[q_spec] + [kv_spec] * len(pieces),
            scratch_shapes=[pltpu.VMEM((len(pieces), 2, head_width, tokens), f32)],
        ),
        out_shape=[jax.ShapeDtypeStruct((rows, tokens), f32)]
        + [jax.ShapeDtypeStruct(p.shape, t) for p, t in zip(pieces, types)],
        input_output_aliases=aliases,
        name="attend_backward",
        cost_estimate=pl.CostEstimate(
            flops=10 * work * head_width, transcendentals=work, bytes_accessed=8 * rows * tokens
        ),
    )(scalars, *operands)


def shift_ctx(value, step):
    size = lax.axis_size("ctx")
    return lax.ppermute(value, "ctx", [(i, (i + step) % size) for i in range(size)])


def swap_dp(value, bit):
    size = lax.axis_size("dp")
    return lax.ppermute(value, "dp", [(i, i ^ bit) for i in range(size)])


def ring_pieces(own):
    size = lax.axis_size("ctx")
    found = [(0, own)]
    up, down = own, own
    for hop in range(1, size // 2 + 1):
        up = shift_ctx(up, 1)
        found.append((-hop, up))
        if hop < size - hop:
            down = shift_ctx(down, -1)
            found.append((hop, down))
    return found


def ring_reduce(parts):
    size = lax.axis_size("ctx")
    top = size // 2
    carry = None
    for hop in range(top, 0, -1):
        piece = parts[-hop]
        if carry is not None:
            piece = (piece.astype(f32) + carry.astype(f32)).astype(bf16)
        carry = shift_ctx(piece, -1)
    total = parts[0].astype(f32) + carry.astype(f32)
    carry = None
    for hop in range(size - top - 1, 0, -1):
        piece = parts[hop]
        if carry is not None:
            piece = (piece.astype(f32) + carry.astype(f32)).astype(bf16)
        carry = shift_ctx(piece, 1)
    if carry is not None:
        total = total + carry.astype(f32)
    return total


def gather_ctx(own):
    size = lax.axis_size("ctx")
    index = lax.axis_index("ctx")
    stack = jnp.zeros((size,) + own.shape, own.dtype)
    for offset, piece in ring_pieces(own):
        stack = lax.dynamic_update_index_in_dim(stack, piece, (index + offset) % size, 0)
    return stack.reshape((size * own.shape[0],) + own.shape[1:])


def gather_dp(block, x_first):
    rows = block.shape[0]
    early, late = (2, 4) if x_first else (4, 2)
    near = swap_dp(block, early)
    far = swap_dp(jnp.concatenate([block, near]), late)
    if x_first:
        half = jnp.concatenate([block, near, far])
    else:
        half = jnp.concatenate([block, far[:rows], near, far[rows:]])
    return jnp.concatenate([half, swap_dp(half, 1)])


def reduce_dp(keep, send, x_first):
    rows = keep.shape[0] // 4
    half = keep.astype(f32) + swap_dp(send, 1).astype(f32)
    if x_first:
        stay, go = half[: 2 * rows], half[2 * rows :]
    else:
        stay = jnp.concatenate([half[:rows], half[2 * rows : 3 * rows]])
        go = jnp.concatenate([half[rows : 2 * rows], half[3 * rows :]])
    early, late = (2, 4) if x_first else (4, 2)
    pair = stay.astype(bf16).astype(f32) + swap_dp(go.astype(bf16), late).astype(f32)
    stay, go = pair[:rows], pair[rows:]
    return stay.astype(bf16).astype(f32) + swap_dp(go.astype(bf16), early).astype(f32)


def reduce_ctx(block):
    size = lax.axis_size("ctx")
    index = lax.axis_index("ctx")
    stack = block.astype(bf16).reshape(size, block.shape[0] // size, block.shape[1])
    parts = {
        offset: lax.dynamic_index_in_dim(stack, (index + offset) % size, 0, keepdims=False)
        for offset in range(-(size // 2), (size - 1) // 2 + 1)
    }
    return ring_reduce(parts)


def to_rel(value):
    count = len(block_bits)
    me = lax.axis_index("dp")
    blocks = value.reshape(count, value.shape[0] // count, value.shape[1])
    picked = [
        lax.dynamic_index_in_dim(blocks, me ^ bits, 0, keepdims=False) for bits in block_bits
    ]
    return jnp.concatenate(picked)


def from_rel(value):
    count = len(block_bits)
    me = lax.axis_index("dp")
    blocks = value.reshape(count, value.shape[0] // count, value.shape[1])
    picked = []
    for owner in range(count):
        bits = me ^ owner
        place = ((bits & 1) << 2) | ((bits >> 1) & 3)
        picked.append(lax.dynamic_index_in_dim(blocks, place, 0, keepdims=False))
    return jnp.concatenate(picked)


def sum_all(value):
    size = lax.axis_size("dp")
    bit = 1
    while bit < size:
        value = value + swap_dp(value, bit)
        bit *= 2
    moved = [value] + [shift_ctx(value, step) for step in range(1, lax.axis_size("ctx"))]
    total = moved[0]
    for piece in moved[1:]:
        total = total + piece
    return total


class RowPlan:
    to_rel = staticmethod(to_rel)
    from_rel = staticmethod(from_rel)
    sum_all = staticmethod(sum_all)

    def gather(self, shards, widths):
        query, key, value, out, gate, up, down = [
            s.reshape(-1, w) for s, w in zip(shards, widths)
        ]
        model = out.shape[1]
        cut = model // 2 // 128 * 128
        kv_width = key.shape[1]
        qkv = gather_ctx(jnp.concatenate([key, value, query], axis=1))
        w_kv = gather_dp(qkv[:, : 2 * kv_width], False)
        w_q = gather_dp(qkv[:, 2 * kv_width :], True)
        o_z = gather_ctx(out)
        w_o = (gather_dp(o_z[:, :cut], True), gather_dp(o_z[:, cut:], False))
        gu = gather_ctx(jnp.concatenate([gate, up], axis=1))
        ff_width = gate.shape[1]
        w_g = gather_dp(gu[:, :ff_width], True)
        w_u = gather_dp(gu[:, ff_width:], False)
        d_z = gather_ctx(down)
        w_d = (gather_dp(d_z[:, :cut], True), gather_dp(d_z[:, cut:], False))
        return w_q, w_kv, jnp.concatenate(w_o, axis=1), w_g, w_u, jnp.concatenate(w_d, axis=1)

    def scatter(self, left, right_t, x_first):
        half = left.shape[0] // 2
        send = dot_nt(left[half:], right_t).astype(bf16)
        keep = dot_nt(left[:half], right_t).astype(bf16)
        return reduce_ctx(reduce_dp(keep, send, x_first)).reshape(-1)


class FlatPlan:
    axes = ("dp", "ctx")

    def to_rel(self, value):
        return value

    def from_rel(self, value):
        return value

    def sum_all(self, value):
        return lax.psum(value, self.axes)

    def gather(self, shards, widths):
        query, key, value, out, gate, up, down = [
            lax.all_gather(s, self.axes, axis=0, tiled=True).reshape(-1, w)
            for s, w in zip(shards, widths)
        ]
        return query, jnp.concatenate([key, value], axis=1), out, gate, up, down

    def scatter(self, left, right_t, x_first):
        whole = dot_nt(left, right_t).reshape(-1)
        return lax.psum_scatter(whole, self.axes, scatter_dimension=0, tiled=True)


def rotary_t(positions, head_width):
    frequency = rope_base ** (-jnp.arange(0, head_width, 2).astype(f32) / head_width)
    angles = frequency[:, None] * positions.astype(f32)[None, :]
    return jnp.cos(angles), jnp.sin(angles)


def rotate_t(value, cosine, sine, head_width):
    rows, tokens = value.shape
    halves = value.reshape(rows // head_width, 2, head_width // 2, tokens)
    first, second = halves[:, 0], halves[:, 1]
    turned = jnp.stack(
        [first * cosine - second * sine, second * cosine + first * sine], axis=1
    )
    return turned.reshape(rows, tokens)


def norm_back(grad, values, inverse, gain):
    scaled = grad * gain[:, None]
    mean = jnp.mean(scaled * values, axis=0, keepdims=True)
    back = inverse * scaled - values * (inverse * inverse * inverse) * mean
    return back, jnp.sum(grad * values * inverse, axis=1)


def per_device(
    tokens,
    cotangent,
    lengths,
    gate_mask,
    block_order,
    w_query,
    w_key,
    w_value,
    w_out,
    w_gate,
    w_up,
    w_down,
    gain_attn,
    gain_mlp,
    w_router,
):
    row_count, model_width = tokens.shape[1:]
    head_width = HEAD_DIM
    group_size = HEADS // KV_HEADS
    kv_width = KV_HEADS * head_width
    q_width = HEADS * head_width
    ctx_size = lax.axis_size("ctx")
    ctx_index = lax.axis_index("ctx")
    shards = (w_query, w_key, w_value, w_out, w_gate, w_up, w_down)
    widths = (q_width, kv_width, kv_width, model_width, FF, FF, model_width)
    by_rows = lax.axis_size("dp") == len(block_bits) and all(
        s.shape[0] % w == 0 for s, w in zip(shards, widths)
    )
    plan = RowPlan() if by_rows else FlatPlan()

    w_q, w_kv, w_o, w_g, w_u, w_d = plan.gather(shards, widths)

    block = row_count // 2
    own_blocks = lax.dynamic_slice_in_dim(block_order, 2 * ctx_index, 2)
    own_pos = (
        own_blocks[:, None] * block + jnp.arange(block, dtype=jnp.int32)[None, :]
    ).reshape(-1)
    seq_length = lengths[0]
    cosine, sine = rotary_t(own_pos, head_width)

    x_t = tokens[0].T.astype(f32)
    inverse_attn = lax.rsqrt(jnp.mean(x_t * x_t, axis=0, keepdims=True) + norm_eps)
    h1 = plan.to_rel((x_t * inverse_attn * gain_attn[:, None]).astype(bf16))
    kv_raw = dot_tn(w_kv, h1)
    k_t = rotate_t(kv_raw[:kv_width], cosine, sine, head_width)
    kv_own = jnp.stack([k_t, kv_raw[kv_width:]]).astype(bf16)
    q_t = rotate_t(dot_tn(w_q, h1), cosine, sine, head_width).astype(bf16) * bf16(
        head_width**-0.5
    )

    found = ring_pieces(kv_own)
    offsets = [offset for offset, _ in found]
    pieces = [piece for _, piece in found]

    def scalars_for(picked):
        blocks = [
            lax.dynamic_slice_in_dim(block_order, 2 * ((ctx_index + o) % ctx_size), 2)
            for o in picked
        ]
        return jnp.concatenate([lengths.astype(jnp.int32), own_blocks] + blocks)

    state = attend_call(scalars_for(offsets[:1]), q_t, pieces[:1], None, False, group_size, head_width)
    if ctx_size > 3:
        state = attend_call(
            scalars_for(offsets[1:3]), q_t, pieces[1:3], state, False, group_size, head_width
        )
    rest = 3 if ctx_size > 3 else 1
    o_t, lse = attend_call(
        scalars_for(offsets[rest:]), q_t, pieces[rest:], state, True, group_size, head_width
    )

    o_rel = plan.to_rel(o_t)
    attn = dot_tn(w_o, o_rel)
    mid = x_t + attn
    inverse_mlp = lax.rsqrt(jnp.mean(mid * mid, axis=0, keepdims=True) + norm_eps)
    h2 = plan.to_rel((mid * inverse_mlp * gain_mlp[:, None]).astype(bf16))
    gate = dot_tn(w_g, h2)
    up = dot_tn(w_u, h2)
    sigmoid = 1.0 / (1.0 + jnp.exp(-gate))
    silu = gate * sigmoid
    hidden = plan.to_rel((silu * up).astype(bf16))
    mlp = dot_tn(w_d, hidden)
    branch = attn + mlp
    router = jax.nn.sigmoid(jnp.sum(x_t * w_router[:, None], axis=0, keepdims=True))
    bits = gate_mask.astype(f32)
    chosen = bits * router
    result = (x_t + chosen * branch).astype(bf16).T

    usable = (own_pos < seq_length).astype(f32)[None, :]
    dy = cotangent[0].T.astype(f32) * usable
    db = dy * chosen
    d_logit = bits * jnp.sum(dy * branch, axis=0, keepdims=True) * router * (1.0 - router)
    grad_router = jnp.sum(d_logit * x_t, axis=1)
    dx = dy + d_logit * w_router[:, None]

    d_mlp = db.astype(bf16)
    grad_down = plan.scatter(hidden, d_mlp, True)
    d_hidden = plan.from_rel(dot_nn(w_d, d_mlp))
    d_gate = (d_hidden * up * (sigmoid * (1.0 + gate * (1.0 - sigmoid)))).astype(bf16)
    d_up = (d_hidden * silu).astype(bf16)
    grad_gate = plan.scatter(h2, d_gate, True)
    grad_up = plan.scatter(h2, d_up, False)
    dh2 = plan.from_rel(dot_nn(w_g, d_gate) + dot_nn(w_u, d_up))
    d_mid, grad_gain_mlp = norm_back(dh2, mid, inverse_mlp, gain_mlp)
    dx = dx + d_mid
    d_attn = (db + d_mid).astype(bf16)
    grad_out = plan.scatter(o_rel, d_attn, False)
    do_t = plan.from_rel(dot_nn(w_o, d_attn).astype(bf16))

    dq = None
    parts = {}
    order = sorted(offsets, key=lambda o: -abs(o))
    for offset in order:
        dq, part = attend_back_call(
            scalars_for([offset]),
            q_t,
            do_t,
            o_t,
            lse,
            [pieces[offsets.index(offset)]],
            dq,
            [bf16 if offset else f32],
            group_size,
            head_width,
        )
        parts[offset] = part
    d_kv = ring_reduce(parts)
    dq_t = rotate_t(dq * head_width**-0.5, cosine, -sine, head_width).astype(bf16)
    dk_t = rotate_t(d_kv[0], cosine, -sine, head_width).astype(bf16)
    dv_t = d_kv[1].astype(bf16)
    dkv_t = jnp.concatenate([dk_t, dv_t])
    grad_query = plan.scatter(h1, dq_t, True)
    grad_key = plan.scatter(h1, dk_t, True)
    grad_value = plan.scatter(h1, dv_t, False)
    dh1 = plan.from_rel(dot_nn(w_q, dq_t) + dot_nn(w_kv, dkv_t))
    d_in, grad_gain_attn = norm_back(dh1, x_t, inverse_attn, gain_attn)
    grad_tokens = (dx + d_in).astype(bf16).T
    small = plan.sum_all(jnp.stack([grad_gain_attn, grad_gain_mlp, grad_router]))
    return (
        result[None],
        grad_tokens[None],
        grad_query,
        grad_key,
        grad_value,
        grad_out,
        grad_gate,
        grad_up,
        grad_down,
        small[0],
        small[1],
        small[2],
    )


def solution(mesh):
    rows = P("dp", "ctx", None)
    flat = P(("dp", "ctx"))
    return jax.shard_map(
        per_device,
        mesh=mesh,
        in_specs=(rows, rows, P("dp"), P("dp", "ctx"), P()) + (flat,) * 7 + (P(),) * 3,
        out_specs=(rows, rows) + (flat,) * 7 + (P(),) * 3,
        check_vma=False,
    )
```

```python
import functools

import jax
import jax.numpy as jnp
from jax import lax
from jax.experimental import pallas as pl
from jax.experimental.layout import Layout, with_layout_constraint
from jax.experimental.pallas import tpu as pltpu
from jax.sharding import PartitionSpec as P

HEADS = 15
KV_HEADS = 5
HEAD_DIM = 64
FF = 2560

norm_eps = 1e-05
rope_base = 100000.0
neg_big = -1e30
f32 = jnp.float32
bf16 = jnp.bfloat16

order_bits = {"x": (0, 2, 4, 6, 1, 3, 5, 7), "y": (0, 4, 2, 6, 1, 5, 3, 7)}
BLOCKS = 8


def dot_nn(left, right):
    return lax.dot_general(left, right, (((1,), (0,)), ((), ())), preferred_element_type=f32)


def dot_tn(left, right):
    return lax.dot_general(left, right, (((0,), (0,)), ((), ())), preferred_element_type=f32)


def dot_nt(left, right):
    return lax.dot_general(left, right, (((1,), (1,)), ((), ())), preferred_element_type=f32)


def attend_body(first, last, places, head_width, group_size, block, sc, *refs):
    pieces = len(places)
    q_ref = refs[0]
    kv_refs = refs[1 : 1 + pieces]
    at = 1 + pieces
    if not first:
        m_in, l_in, acc_in = refs[at : at + 3]
        at += 3
    if last:
        o_ref, lse_ref = refs[at : at + 2]
        at += 2
        m_ref, l_ref, acc_ref = refs[at : at + 3]
    else:
        m_out, l_out, acc_out = refs[at : at + 3]
        m_ref, l_ref, acc_ref = m_out.at[0], l_out.at[0], acc_out.at[0]
    length = sc[0]
    width = group_size * block
    for qb in range(2):
        q_blk = sc[1 + qb]
        cols = slice(qb * block, (qb + 1) * block)
        q_cat = jnp.concatenate(
            [q_ref[h * head_width : (h + 1) * head_width, cols] for h in range(group_size)], axis=1
        )
        if first:
            m_ref[qb : qb + 1, :] = jnp.full((1, width), neg_big, f32)
            l_ref[qb : qb + 1, :] = jnp.zeros((1, width), f32)
            acc_ref[qb] = jnp.zeros((head_width, width), f32)
        else:
            m_ref[qb : qb + 1, :] = m_in[0, qb : qb + 1, :]
            l_ref[qb : qb + 1, :] = l_in[0, qb : qb + 1, :]
            acc_ref[qb] = acc_in[0, qb]
        for piece in range(pieces):
            for sub in range(2):
                k_blk = sc[1 + 2 * places[piece] + sub]
                start = k_blk * block
                keys = slice(sub * block, (sub + 1) * block)

                def step(masked, piece=piece, keys=keys, k_blk=k_blk, start=start):
                    key_t = kv_refs[piece][0, :, keys]
                    val_t = kv_refs[piece][1, :, keys]
                    scores = dot_tn(key_t, q_cat)
                    if masked:
                        k_pos = start + lax.broadcasted_iota(jnp.int32, (block, block), 0)
                        q_pos = q_blk * block + lax.broadcasted_iota(jnp.int32, (block, block), 1)
                        seen = (k_pos <= q_pos) & (k_pos < length)
                        scores = jnp.concatenate(
                            [
                                jnp.where(seen, scores[:, h * block : (h + 1) * block], neg_big)
                                for h in range(group_size)
                            ],
                            axis=1,
                        )
                    m_old = m_ref[qb : qb + 1, :]
                    m_new = jnp.maximum(m_old, jnp.max(scores, axis=0, keepdims=True))
                    probs = jnp.exp(scores - m_new)
                    alpha = jnp.exp(m_old - m_new)
                    m_ref[qb : qb + 1, :] = m_new
                    l_ref[qb : qb + 1, :] = alpha * l_ref[qb : qb + 1, :] + jnp.sum(
                        probs, axis=0, keepdims=True
                    )
                    acc_ref[qb] = acc_ref[qb] * alpha + dot_nn(val_t, probs.astype(bf16))

                live = (k_blk <= q_blk) & (start < length)
                plain = (k_blk < q_blk) & (start + block <= length)
                pl.when(plain)(functools.partial(step, False))
                pl.when(live & jnp.logical_not(plain))(functools.partial(step, True))
        if last:
            total = l_ref[qb : qb + 1, :]
            out = acc_ref[qb] * (1.0 / total)
            for h in range(group_size):
                o_ref[h * head_width : (h + 1) * head_width, cols] = out[
                    :, h * block : (h + 1) * block
                ].astype(bf16)
            lse_ref[0, qb : qb + 1, :] = m_ref[qb : qb + 1, :] + jnp.log(total)


def attend_call(scalars, places, q_t, pieces, state, last, group_size, head_width):
    rows, tokens = q_t.shape
    kv_count = rows // (group_size * head_width)
    block = tokens // 2
    width = group_size * block
    first = state is None
    q_spec = pl.BlockSpec((group_size * head_width, tokens), lambda g, sc: (g, 0))
    kv_spec = pl.BlockSpec((2, head_width, tokens), lambda g, sc: (0, g, 0))
    row_spec = pl.BlockSpec((1, 2, width), lambda g, sc: (g, 0, 0))
    acc_spec = pl.BlockSpec((1, 2, head_width, width), lambda g, sc: (g, 0, 0, 0))
    row_shape = jax.ShapeDtypeStruct((kv_count, 2, width), f32)
    acc_shape = jax.ShapeDtypeStruct((kv_count, 2, head_width, width), f32)
    in_specs = [q_spec] + [kv_spec] * len(pieces)
    operands = [q_t] + list(pieces)
    aliases = {}
    if not first:
        in_specs += [row_spec, row_spec, acc_spec]
        operands += list(state)
    if last:
        out_specs = [q_spec, row_spec]
        out_shape = [jax.ShapeDtypeStruct((rows, tokens), bf16), row_shape]
        scratch = [
            pltpu.VMEM((2, width), f32),
            pltpu.VMEM((2, width), f32),
            pltpu.VMEM((2, head_width, width), f32),
        ]
    else:
        out_specs = [row_spec, row_spec, acc_spec]
        out_shape = [row_shape, row_shape, acc_shape]
        scratch = []
    body = functools.partial(
        attend_body, first, last, places, head_width, group_size, block
    )
    return pl.pallas_call(
        body,
        grid_spec=pltpu.PrefetchScalarGridSpec(
            num_scalar_prefetch=1,
            grid=(kv_count,),
            in_specs=in_specs,
            out_specs=out_specs,
            scratch_shapes=scratch,
        ),
        out_shape=out_shape,
        input_output_aliases=aliases,
        name="attend_forward",
    )(scalars, *operands)


def attend_back_body(first, places, head_width, group_size, block, sc, *refs):
    pieces = len(places)
    q_ref, do_ref, o_ref, lse_ref = refs[:4]
    kv_refs = refs[4 : 4 + pieces]
    at = 4 + pieces
    if not first:
        dq_in = refs[at]
        at += 1
    dq_ref = refs[at]
    dkv_refs = refs[at + 1 : at + 1 + pieces]
    dkv_acc = refs[at + 1 + pieces]
    length = sc[0]
    dkv_acc[...] = jnp.zeros(dkv_acc.shape, f32)
    if first:
        dq_ref[...] = jnp.zeros(dq_ref.shape, f32)
    else:
        dq_ref[...] = dq_in[...]
    for qb in range(2):
        q_blk = sc[1 + qb]
        cols = slice(qb * block, (qb + 1) * block)

        def side_by_side(ref, cols=cols):
            return jnp.concatenate(
                [ref[h * head_width : (h + 1) * head_width, cols] for h in range(group_size)],
                axis=1,
            )

        q_cat = side_by_side(q_ref)
        do_cat = side_by_side(do_ref)
        o_cat = side_by_side(o_ref)
        delta = jnp.sum(do_cat.astype(f32) * o_cat.astype(f32), axis=0, keepdims=True)
        lse = lse_ref[0, qb : qb + 1, :]
        for piece in range(pieces):
            for sub in range(2):
                k_blk = sc[1 + 2 * places[piece] + sub]
                start = k_blk * block
                keys = slice(sub * block, (sub + 1) * block)

                def step(
                    masked, piece=piece, keys=keys, start=start, q_blk=q_blk, q_cat=q_cat,
                    do_cat=do_cat, delta=delta, lse=lse, cols=cols,
                ):
                    key_t = kv_refs[piece][0, :, keys]
                    val_t = kv_refs[piece][1, :, keys]
                    scores = dot_tn(key_t, q_cat)
                    if masked:
                        k_pos = start + lax.broadcasted_iota(jnp.int32, (block, block), 0)
                        q_pos = q_blk * block + lax.broadcasted_iota(jnp.int32, (block, block), 1)
                        seen = (k_pos <= q_pos) & (k_pos < length)
                        scores = jnp.concatenate(
                            [
                                jnp.where(seen, scores[:, h * block : (h + 1) * block], neg_big)
                                for h in range(group_size)
                            ],
                            axis=1,
                        )
                    probs = jnp.exp(scores - lse)
                    d_probs = dot_tn(val_t, do_cat)
                    d_scores = (probs * (d_probs - delta)).astype(bf16)
                    dkv_acc[piece, 1, :, keys] += dot_nt(do_cat, probs.astype(bf16))
                    dkv_acc[piece, 0, :, keys] += dot_nt(q_cat, d_scores)
                    dq = dot_nn(key_t, d_scores)
                    for h in range(group_size):
                        dq_ref[h * head_width : (h + 1) * head_width, cols] += dq[
                            :, h * block : (h + 1) * block
                        ]

                live = (k_blk <= q_blk) & (start < length)
                plain = (k_blk < q_blk) & (start + block <= length)
                pl.when(plain)(functools.partial(step, False))
                pl.when(live & jnp.logical_not(plain))(functools.partial(step, True))
    for piece in range(pieces):
        dkv_refs[piece][...] = dkv_acc[piece].astype(dkv_refs[piece].dtype)


def attend_back_call(
    scalars, places, q_t, do_t, o_t, lse, pieces, dq_before, types, group_size, head_width
):
    rows, tokens = q_t.shape
    kv_count = rows // (group_size * head_width)
    block = tokens // 2
    width = group_size * block
    first = dq_before is None
    q_spec = pl.BlockSpec((group_size * head_width, tokens), lambda g, sc: (g, 0))
    kv_spec = pl.BlockSpec((2, head_width, tokens), lambda g, sc: (0, g, 0))
    row_spec = pl.BlockSpec((1, 2, width), lambda g, sc: (g, 0, 0))
    in_specs = [q_spec, q_spec, q_spec, row_spec] + [kv_spec] * len(pieces)
    operands = [q_t, do_t, o_t, lse] + list(pieces)
    aliases = {}
    if not first:
        in_specs.append(q_spec)
        operands.append(dq_before)
        aliases = {len(operands): 0}
    body = functools.partial(attend_back_body, first, places, head_width, group_size, block)
    return pl.pallas_call(
        body,
        grid_spec=pltpu.PrefetchScalarGridSpec(
            num_scalar_prefetch=1,
            grid=(kv_count,),
            in_specs=in_specs,
            out_specs=[q_spec] + [kv_spec] * len(pieces),
            scratch_shapes=[pltpu.VMEM((len(pieces), 2, head_width, tokens), f32)],
        ),
        out_shape=[jax.ShapeDtypeStruct((rows, tokens), f32)]
        + [jax.ShapeDtypeStruct(p.shape, t) for p, t in zip(pieces, types)],
        input_output_aliases=aliases,
        name="attend_backward",
    )(scalars, *operands)


def ring_order(size):
    return list(range(0, size, 2)) + list(range(1, size, 2))[::-1]


def ring_member(offset):
    size = lax.axis_size("ctx")
    index = lax.axis_index("ctx")
    place = jnp.where(index % 2 == 0, index // 2, size - 1 - index // 2)
    there = (place + offset) % size
    return jnp.where(2 * there < size, 2 * there, 2 * (size - 1 - there) + 1)


def shift_ctx(value, step):
    order = ring_order(lax.axis_size("ctx"))
    size = len(order)
    return lax.ppermute(
        value, "ctx", [(order[i], order[(i + step) % size]) for i in range(size)]
    )


def swap_dp(value, bit):
    size = lax.axis_size("dp")
    return lax.ppermute(value, "dp", [(i, i ^ bit) for i in range(size)])


class Job:
    def __init__(self, steps):
        self.steps = steps
        self.pending = None
        self.result = None
        self.done = False
        self.advance(None)

    def advance(self, arrived):
        if self.done:
            return
        try:
            self.pending = self.steps.send(arrived)
        except StopIteration as stop:
            self.done, self.pending, self.result = True, None, stop.value

    def finish(self):
        while not self.done:
            self.advance(self.pending)
        return self.result


def tick(values, *jobs):
    live = [job for job in jobs if not job.done]
    values, arrived = lax.optimization_barrier((values, [job.pending for job in live]))
    for job, got in zip(live, arrived):
        job.advance(got)
    return values


def ring_steps(own, found):
    size = lax.axis_size("ctx")
    found.append((0, own))
    up, down = own, own
    for hop in range(1, size // 2 + 1):
        if hop < size - hop:
            up, down = yield [shift_ctx(up, 1), shift_ctx(down, -1)]
            found += [(-hop, up), (hop, down)]
        else:
            (up,) = yield [shift_ctx(up, 1)]
            found.append((-hop, up))
    return found


def gather_ctx_steps(arrays):
    widths = [a.shape[1] for a in arrays]
    own = jnp.concatenate(arrays, axis=1) if len(arrays) > 1 else arrays[0]
    size = lax.axis_size("ctx")
    found = yield from ring_steps(own, [])
    stack = jnp.zeros((size,) + own.shape, own.dtype)
    for offset, piece in found:
        stack = lax.dynamic_update_index_in_dim(stack, piece, ring_member(offset), 0)
    whole = stack.reshape(size * own.shape[0], own.shape[1])
    cuts = [sum(widths[:i]) for i in range(len(widths) + 1)]
    return [whole[:, lo:hi] for lo, hi in zip(cuts[:-1], cuts[1:])]


def stack_body(*refs):
    rows = refs[0].shape[0]
    for i, ref in enumerate(refs[:-1]):
        refs[-1][i * rows : (i + 1) * rows, :] = ref[...]


def stack_call(pieces):
    rows, width = pieces[0].shape
    lanes = 512 if width % 512 == 0 else width
    return pl.pallas_call(
        stack_body,
        grid=(width // lanes,),
        in_specs=[pl.BlockSpec((rows, lanes), lambda i: (0, i))] * len(pieces),
        out_specs=pl.BlockSpec((rows * len(pieces), lanes), lambda i: (0, i)),
        out_shape=jax.ShapeDtypeStruct((rows * len(pieces), width), pieces[0].dtype),
        name="stack",
    )(*pieces)


def gather_dp_steps(units):
    links = [order_bits[order][1:3] for _, order in units]
    blocks = [block for block, _ in units]
    first = yield [
        [swap_dp(b, early), swap_dp(b, late), swap_dp(b, 1)]
        for b, (early, late) in zip(blocks, links)
    ]
    second = yield [
        [swap_dp(near, late), swap_dp(near, 1), swap_dp(far, 1)]
        for (near, far, _), (_, late) in zip(first, links)
    ]
    third = yield [[swap_dp(corner, 1)] for corner, _, _ in second]
    return [
        stack_call([b, near, far, corner, b_o, near_o, far_o, corner_o])
        for b, (near, far, b_o), (corner, near_o, far_o), (corner_o,) in zip(
            blocks, first, second, third
        )
    ]


def reduce_dp_steps(units):
    got = yield [swap_dp(send, 1) for _, send, _ in units]
    stays = [keep for keep, _, _ in units]
    links = [order_bits[order][1:3] for _, _, order in units]
    for level in (1, 0):
        rows = [s.shape[0] // 2 for s in stays]
        goes = [
            (s[r:].astype(f32) + g[r:].astype(f32)).astype(bf16)
            for s, g, r in zip(stays, got, rows)
        ]
        moving = [swap_dp(go, link[level]) for go, link in zip(goes, links)]
        stays = [
            (s[:r].astype(f32) + g[:r].astype(f32)).astype(bf16)
            for s, g, r in zip(stays, got, rows)
        ]
        got = yield moving
    return [(s.astype(f32) + g.astype(f32)).astype(bf16) for s, g in zip(stays, got)]


def reduce_ring_steps(parts):
    size = lax.axis_size("ctx")
    top = size // 2
    total = parts[0].astype(f32)
    up = down = None
    for hop in range(top, 0, -1):
        pieces = [(parts[-hop], up, -1)]
        if hop < size - hop:
            pieces.append((parts[hop], down, 1))
        moving = []
        for piece, carry, step in pieces:
            if carry is not None:
                piece = (piece.astype(f32) + carry.astype(f32)).astype(bf16)
            moving.append(shift_ctx(piece, step))
        got = yield moving
        up = got[0]
        down = got[1] if len(got) > 1 else None
    total = total + up.astype(f32)
    return total if down is None else total + down.astype(f32)


def reduce_ctx_steps(blocks):
    size = lax.axis_size("ctx")
    widths = [b.shape[1] for b in blocks]
    whole = jnp.concatenate(blocks, axis=1) if len(blocks) > 1 else blocks[0]
    stack = whole.reshape(size, whole.shape[0] // size, whole.shape[1])
    parts = {
        offset: lax.dynamic_index_in_dim(stack, ring_member(offset), 0, keepdims=False)
        for offset in range(-(size // 2), (size - 1) // 2 + 1)
    }
    total = yield from reduce_ring_steps(parts)
    cuts = [sum(widths[:i]) for i in range(len(widths) + 1)]
    return [total[:, lo:hi].reshape(-1) for lo, hi in zip(cuts[:-1], cuts[1:])]


def sum_all_steps(value):
    bit = 1
    while bit < lax.axis_size("dp"):
        (got,) = yield [swap_dp(value, bit)]
        value = value + got
        bit *= 2
    moved = yield [shift_ctx(value, step) for step in range(1, lax.axis_size("ctx"))]
    for piece in moved:
        value = value + piece
    return value


LANES = 256


def blocked(value):
    return value.reshape((BLOCKS, value.shape[0] // BLOCKS) + value.shape[1:])


def tile_spec(shape):
    zeros = (0,) * (len(shape) - 1)
    return pl.BlockSpec(tuple(shape[:-1]) + (LANES,), lambda t, index: zeros + (t,))


def whole_spec(shape):
    zeros = (0,) * len(shape)
    return pl.BlockSpec(tuple(shape), lambda t, index: zeros)


def token_call(body, name, index, inputs, outputs, fixed_in=(), fixed_out=()):
    tokens = inputs[0].shape[-1]
    return pl.pallas_call(
        body,
        grid_spec=pltpu.PrefetchScalarGridSpec(
            num_scalar_prefetch=1,
            grid=(tokens // LANES,),
            in_specs=[tile_spec(a.shape) for a in inputs] + [whole_spec(a.shape) for a in fixed_in],
            out_specs=[tile_spec(o.shape) for o in outputs]
            + [whole_spec(o.shape) for o in fixed_out],
        ),
        out_shape=list(outputs) + list(fixed_out),
        name=name,
    )(index, *inputs, *fixed_in)


def norm_body(orders, added, width, index, *refs):
    count = 2 if added else 1
    x_ref = refs[0]
    gain_ref = refs[count]
    outs = refs[count + 1 :]
    inverse_ref = outs[0]
    h_refs = outs[1 : 1 + len(orders)]
    values = x_ref
    total = None
    if added:
        values = outs[1 + len(orders)]
    for i in range(BLOCKS):
        part = x_ref[i].astype(f32)
        if added:
            part = part + refs[1][i]
            values[i] = part
        square = jnp.sum(part * part, axis=0, keepdims=True)
        total = square if total is None else total + square
    inverse = lax.rsqrt(total * (1.0 / width) + norm_eps)
    inverse_ref[...] = inverse
    for at, h_ref in zip(orders, h_refs):
        for i in range(BLOCKS):
            j = index[at * BLOCKS + i]
            h_ref[i] = (values[j].astype(f32) * inverse * gain_ref[j]).astype(bf16)


def norm_call(index, orders, x, added, gain):
    x3 = blocked(x)
    inputs = [x3] + ([blocked(added)] if added is not None else [])
    outputs = [jax.ShapeDtypeStruct((1, x.shape[1]), f32)]
    outputs += [jax.ShapeDtypeStruct(x3.shape, bf16)] * len(orders)
    if added is not None:
        outputs.append(jax.ShapeDtypeStruct(x3.shape, f32))
    body = functools.partial(norm_body, orders, added is not None, x.shape[0])
    got = token_call(body, "norm", index, inputs, outputs, [blocked(gain[:, None])])
    return [got[0]] + [g.reshape(x.shape) for g in got[1:]]


def norm_back_body(at_list, width, extras, index, *refs):
    count = len(at_list)
    grads = refs[:count]
    values, inverse_ref = refs[count : count + 2]
    extra_refs = refs[count + 2 : count + 2 + extras]
    gain_ref = refs[count + 2 + extras]
    outs = refs[count + 3 + extras : count + 3 + 2 * extras]
    sum_ref = refs[count + 3 + 2 * extras]
    inverse = inverse_ref[...]

    def grad_of(i):
        total = None
        for at, ref in zip(at_list, grads):
            part = ref[index[at * BLOCKS + i]]
            total = part if total is None else total + part
        return total

    @pl.when(pl.program_id(0) == 0)
    def _():
        sum_ref[...] = jnp.zeros(sum_ref.shape, f32)

    mean = None
    for i in range(BLOCKS):
        along = grad_of(i) * values[i].astype(f32)
        sum_ref[i] += jnp.sum(along * inverse, axis=1, keepdims=True)
        part = jnp.sum(along * gain_ref[i], axis=0, keepdims=True)
        mean = part if mean is None else mean + part
    factor = mean * (1.0 / width) * (inverse * inverse * inverse)
    for i in range(BLOCKS):
        back = inverse * (grad_of(i) * gain_ref[i]) - values[i].astype(f32) * factor
        for extra, out in zip(extra_refs, outs):
            out[i] = (extra[i] + back).astype(out.dtype)


def norm_back_call(index, grads, values, inverse, gain, extras):
    shape = values.shape
    inputs = [blocked(g) for g, _ in grads] + [blocked(values), inverse]
    inputs += [blocked(e) for e, _ in extras]
    outputs = [jax.ShapeDtypeStruct(blocked(values).shape, t) for _, t in extras]
    column = blocked(gain[:, None])
    body = functools.partial(norm_back_body, [at for _, at in grads], shape[0], len(extras))
    got = token_call(
        body, "norm_back", index, inputs, outputs, [column],
        [jax.ShapeDtypeStruct(column.shape, f32)],
    )
    return [g.reshape(shape) for g in got[:-1]] + [got[-1].reshape(shape[0])]


def pick_body(at, index, in_ref, out_ref):
    for i in range(BLOCKS):
        out_ref[i] = in_ref[index[at * BLOCKS + i]]


def pick_call(index, at, value):
    three = blocked(value)
    (out,) = token_call(
        functools.partial(pick_body, at), "pick", index, [three],
        [jax.ShapeDtypeStruct(three.shape, value.dtype)],
    )
    return out.reshape(value.shape)


def silu_body(parts, index, gate_ref, up_ref, *outs):
    for part in range(parts):
        for i in range(BLOCKS):
            j = index[part * BLOCKS + i]
            gate = gate_ref[j, part]
            outs[part][i] = (gate * up_ref[j, part] / (1.0 + jnp.exp(-gate))).astype(bf16)


def in_parts(value, parts):
    rows, tokens = value.shape
    return value.reshape(BLOCKS, parts, rows // (BLOCKS * parts), tokens)


def silu_call(index, parts, gate, up):
    rows, tokens = gate.shape
    shape = (BLOCKS, rows // (BLOCKS * parts), tokens)
    got = token_call(
        functools.partial(silu_body, parts), "silu", index,
        [in_parts(gate, parts), in_parts(up, parts)],
        [jax.ShapeDtypeStruct(shape, bf16)] * parts,
    )
    return [g.reshape(rows // parts, tokens) for g in got]


def silu_back_body(parts, index, gate_ref, up_ref, *refs):
    grads, outs = refs[:parts], refs[parts:]
    for part in range(parts):
        for i in range(BLOCKS):
            grad = grads[part][index[part * BLOCKS + i]]
            gate = gate_ref[i, part]
            sigmoid = 1.0 / (1.0 + jnp.exp(-gate))
            slope = sigmoid * (1.0 + gate * (1.0 - sigmoid))
            outs[0][i, part] = (grad * up_ref[i, part] * slope).astype(bf16)
            outs[1][i, part] = (grad * (gate * sigmoid)).astype(bf16)


def silu_back_call(index, gate, up, grads):
    parts = len(grads)
    views = [in_parts(gate, parts), in_parts(up, parts)]
    got = token_call(
        functools.partial(silu_back_body, parts), "silu_back", index,
        views + [blocked(g) for g in grads],
        [jax.ShapeDtypeStruct(views[0].shape, bf16)] * 2,
    )
    return [g.reshape(gate.shape) for g in got]


def row_major(value):
    return with_layout_constraint(value, Layout(major_to_minor=(0, 1)))


class RowPlan:
    parts = 2

    def indices(self):
        me = lax.axis_index("dp")
        own = me ^ jnp.array(order_bits["x"] + order_bits["y"], jnp.int32)
        at = jnp.arange(2 * BLOCKS, dtype=jnp.int32)
        bits = me ^ (at % BLOCKS)
        in_x = ((bits & 1) << 2) | ((bits >> 1) & 3)
        in_y = ((bits & 1) << 2) | (bits & 2) | ((bits >> 2) & 1)
        return own, jnp.where(at < BLOCKS, in_x, in_y)

    def sum_all(self, value):
        return Job(sum_all_steps(value))

    def gather_ctx(self, arrays):
        return Job(gather_ctx_steps(arrays))

    def gather_dp(self, *units):
        return Job(gather_dp_steps(units))

    def row_parts(self, block):
        rows = block.shape[0] // self.parts
        return [block[i * rows : (i + 1) * rows] for i in range(self.parts)]

    def halves(self, left, right_t):
        half = left.shape[0] // 2
        send = row_major(dot_nt(left[half:], right_t).astype(bf16))
        keep = row_major(dot_nt(left[:half], right_t).astype(bf16))
        return keep, send

    def reduce_dp(self, *units):
        return Job(reduce_dp_steps(units))

    def reduce_ctx(self, blocks):
        return Job(reduce_ctx_steps(blocks))


def at_once(result):
    return result
    yield


class FlatPlan:
    axes = ("dp", "ctx")
    parts = 1

    def indices(self):
        plain = jnp.concatenate([jnp.arange(BLOCKS, dtype=jnp.int32)] * 2)
        return plain, plain

    def sum_all(self, value):
        return Job(at_once(lax.psum(value, self.axes)))

    def gather_ctx(self, arrays):
        return Job(
            at_once(
                [
                    lax.all_gather(a.flat, self.axes, axis=0, tiled=True).reshape(-1, a.width)
                    for a in arrays
                ]
            )
        )

    def gather_dp(self, *units):
        return Job(at_once([block for block, _ in units]))

    def row_parts(self, block):
        return [block]

    def halves(self, left, right_t):
        return dot_nt(left, right_t), None

    def reduce_dp(self, *units):
        return Job(at_once([keep for keep, _, _ in units]))

    def reduce_ctx(self, blocks):
        return Job(
            at_once(
                [
                    lax.psum_scatter(b.reshape(-1), self.axes, scatter_dimension=0, tiled=True)
                    for b in blocks
                ]
            )
        )


@jax.tree_util.register_pytree_node_class
class FlatShard:
    def __init__(self, flat, width):
        self.flat, self.width = flat, width

    def tree_flatten(self):
        return (self.flat,), self.width

    @classmethod
    def tree_unflatten(cls, width, leaves):
        return cls(leaves[0], width)


def rotary_t(positions, head_width):
    frequency = rope_base ** (-jnp.arange(0, head_width, 2).astype(f32) / head_width)
    angles = frequency[:, None] * positions.astype(f32)[None, :]
    return jnp.cos(angles), jnp.sin(angles)


def rotate_t(value, cosine, sine, head_width):
    rows, tokens = value.shape
    halves = value.reshape(rows // head_width, 2, head_width // 2, tokens)
    first, second = halves[:, 0], halves[:, 1]
    turned = jnp.stack(
        [first * cosine - second * sine, second * cosine + first * sine], axis=1
    )
    return turned.reshape(rows, tokens)


def per_device(
    tokens,
    cotangent,
    lengths,
    gate_mask,
    block_order,
    w_query,
    w_key,
    w_value,
    w_out,
    w_gate,
    w_up,
    w_down,
    gain_attn,
    gain_mlp,
    w_router,
):
    row_count, model_width = tokens.shape[1:]
    head_width = HEAD_DIM
    group_size = HEADS // KV_HEADS
    kv_width = KV_HEADS * head_width
    q_width = HEADS * head_width
    ctx_size = lax.axis_size("ctx")
    ctx_index = lax.axis_index("ctx")
    shards = (w_query, w_key, w_value, w_out, w_gate, w_up, w_down)
    widths = (q_width, kv_width, kv_width, model_width, FF, FF, model_width)
    by_rows = lax.axis_size("dp") == BLOCKS and all(
        s.shape[0] % w == 0 for s, w in zip(shards, widths)
    )
    plan = RowPlan() if by_rows else FlatPlan()
    wrap = (lambda s, w: s.reshape(-1, w)) if by_rows else FlatShard
    s_q, s_k, s_v = [wrap(s, w) for s, w in zip(shards[:3], widths[:3])]

    z_qkv = plan.gather_ctx([s_k, s_v, s_q])
    later = (tokens, lengths, block_order, gain_attn, gain_mlp) + shards[3:]
    later = tick(later, z_qkv)
    tokens, lengths, block_order, gain_attn, gain_mlp = later[:5]
    s_o, s_g, s_u, s_d = later[5:]
    own_at, abs_at = plan.indices()
    x_t = tokens[0].T
    inverse_attn, h1x, h1y = norm_call(own_at, (0, 1), x_t, None, gain_attn)
    s_g, s_o, h1x, h1y = tick((s_g, s_o, h1x, h1y), z_qkv)
    z_k, z_v, z_q = z_qkv.finish()
    dp_qkv = plan.gather_dp((jnp.concatenate([z_k, z_v], axis=1), "y"), (z_q, "x"))
    zj_g = plan.gather_ctx([wrap(s_g, FF)])
    s_u, s_o = tick((s_u, s_o), dp_qkv, zj_g)
    zj_o = plan.gather_ctx([wrap(s_o, model_width)])
    block = row_count // 2
    own_rows = 2 * ctx_index + jnp.arange(2, dtype=jnp.int32)
    own_pos = (
        block_order[own_rows][:, None] * block + jnp.arange(block, dtype=jnp.int32)[None, :]
    ).reshape(-1)
    cosine, sine = rotary_t(own_pos, head_width)
    offsets = [0]
    for hop in range(1, ctx_size // 2 + 1):
        offsets += [-hop, hop] if hop < ctx_size - hop else [-hop]
    held = jnp.concatenate(
        [2 * ring_member(o) + jnp.arange(2, dtype=jnp.int32) for o in offsets]
    )
    scalars = jnp.concatenate([lengths.astype(jnp.int32), block_order[held]])
    seq_length = lengths[0]
    s_u, cosine, sine, scalars = tick((s_u, cosine, sine, scalars), dp_qkv, zj_g, zj_o)
    (z_g,) = zj_g.finish()
    zj_u = plan.gather_ctx([wrap(s_u, FF)])
    s_d, h1x, h1y, z_g = tick((s_d, h1x, h1y, z_g), dp_qkv)
    w_kv, w_q = dp_qkv.finish()

    kv_raw = dot_tn(w_kv, h1y)
    k_t = rotate_t(kv_raw[:kv_width], cosine, sine, head_width)
    kv_own = jnp.stack([k_t, kv_raw[kv_width:]]).astype(bf16)
    kv_found = []
    kv_ring = Job(ring_steps(kv_own, kv_found))
    q_t = rotate_t(dot_tn(w_q, h1x), cosine, sine, head_width).astype(bf16) * bf16(
        head_width**-0.5
    )
    dp_g = plan.gather_dp((z_g, "x"))
    q_t, s_d = tick((q_t, s_d), zj_u, zj_o)
    (z_o,) = zj_o.finish()
    dp_o = plan.gather_dp((z_o, "y"))

    def attend(at, pieces, state, last):
        return attend_call(scalars, at, q_t, pieces, state, last, group_size, head_width)

    if by_rows and ctx_size == 4:
        state = attend([0], [kv_own], None, False)
        state, q_t, s_d = tick((state, q_t, s_d), zj_u, dp_g)
        (z_u,) = zj_u.finish()
        dp_u = plan.gather_dp((z_u, "y"))
        state, q_t, s_d = tick((state, q_t, s_d), kv_ring, dp_o)
        z_d = plan.gather_ctx([wrap(s_d, model_width)])
        state = attend([1, 2], [kv for _, kv in kv_found[1:]], state, False)
        state, q_t = tick((state, q_t), kv_ring, dp_o, dp_u, dp_g)
        found = kv_ring.finish()
        o_t, lse = attend([3], [found[3][1]], state, True)
        o_t, lse, q_t = tick((o_t, lse, q_t), z_d, dp_o, dp_u)
    else:
        z_u, dp_u = zj_u.finish(), None
        dp_u = plan.gather_dp((z_u[0], "y"))
        z_d = plan.gather_ctx([wrap(s_d, model_width)])
        found = kv_ring.finish()
        o_t, lse = attend(list(range(len(found))), [kv for _, kv in found], None, True)
    pieces = [piece for _, piece in found]
    d_orders = ("x", "y")[: plan.parts]
    (w_o,) = dp_o.finish()

    o_rel = pick_call(own_at, 1, o_t)
    attn = dot_tn(w_o, o_rel)
    x_t, attn = tick((x_t, attn), z_d)
    (d_block,) = z_d.finish()
    dp_d = plan.gather_dp(*zip(plan.row_parts(d_block), d_orders))
    inverse_mlp, h2x, h2y, mid = norm_call(own_at, (0, 1), x_t, attn, gain_mlp)
    h2x, h2y, attn = tick((h2x, h2y, attn), dp_u)
    (w_g,) = dp_g.finish()
    (w_u,) = dp_u.finish()
    gate = dot_tn(w_g, h2x)
    gate, h2y = tick((gate, h2y), dp_d)
    up = dot_tn(w_u, h2y)
    gate, up, w_g, w_u = tick((gate, up, w_g, w_u), dp_d)
    hidden = silu_call(own_at, plan.parts, gate, up)
    hidden = tick(hidden, dp_d)
    w_d = dp_d.finish()

    x_f = x_t.astype(f32)
    router = jax.nn.sigmoid(jnp.sum(x_f * w_router[:, None], axis=0, keepdims=True))
    bits = gate_mask.astype(f32)
    chosen = bits * router
    usable = (own_pos < seq_length).astype(f32)[None, :]
    dy = cotangent[0].T.astype(f32) * usable
    db = dy * chosen
    d_mlp = db.astype(bf16)
    r_d = plan.reduce_dp(*[(*plan.halves(h, d_mlp), o) for h, o in zip(hidden, d_orders)])
    d_hidden = [dot_nn(w, d_mlp) for w in w_d]
    mlp = sum(dot_tn(w, h) for w, h in zip(w_d, hidden))
    branch = attn + mlp
    result = (x_f + chosen * branch).astype(bf16).T
    d_logit = bits * jnp.sum(dy * branch, axis=0, keepdims=True) * router * (1.0 - router)
    grad_router = jnp.sum(d_logit * x_f, axis=1)
    d_hidden, d_mlp = tick((d_hidden, d_mlp), r_d)
    d_gate, d_up = silu_back_call(abs_at, gate, up, d_hidden)
    both_g = plan.halves(h2x, d_gate)
    both_u = plan.halves(h2y, d_up)
    d_gate, d_up, both_g, both_u, mlp = tick((d_gate, d_up, both_g, both_u, mlp), r_d)
    r_gu = plan.reduce_dp((*both_g, "x"), (*both_u, "y"))
    dh2x = dot_nn(w_g, d_gate)
    dh2y = dot_nn(w_u, d_up)
    dx = dy + d_logit * w_router[:, None]
    dh2x, dh2y, dx, result, grad_router = tick((dh2x, dh2y, dx, result, grad_router), r_d, r_gu)
    d_blocks = r_d.finish()
    zr_d = plan.reduce_ctx([jnp.concatenate(d_blocks) if len(d_blocks) > 1 else d_blocks[0]])
    dx, d_attn, grad_gain_mlp = norm_back_call(
        abs_at, [(dh2x, 0), (dh2y, 1)], mid, inverse_mlp, gain_mlp, [(dx, f32), (db, bf16)]
    )
    do_t = pick_call(abs_at, 1, dot_nn(w_o, d_attn).astype(bf16))
    both_o = plan.halves(o_rel, d_attn)
    do_t, both_o, dx, grad_gain_mlp = tick((do_t, both_o, dx, grad_gain_mlp), zr_d)
    r_o = plan.reduce_dp((*both_o, "y"))

    def attend_back(offset, dq):
        dq, part = attend_back_call(
            scalars,
            [offsets.index(offset)],
            q_t,
            do_t,
            o_t,
            lse,
            [pieces[offsets.index(offset)]],
            dq,
            [bf16 if offset else f32],
            group_size,
            head_width,
        )
        return dq, part

    dq = None
    if by_rows and ctx_size == 4:
        dq, far = attend_back(-2, None)
        dq, far, do_t, dx = tick((dq, far, do_t, dx), zr_d, r_o)
        far_moving = shift_ctx(far, -1)
        dq, back = attend_back(-1, dq)
        dq, back, far_moving, do_t = tick((dq, back, far_moving, do_t), r_gu)
        back = (back.astype(f32) + far_moving.astype(f32)).astype(bf16)
        back_moving = shift_ctx(back, -1)
        dq, ahead = attend_back(1, dq)
        dq, ahead, back_moving, do_t = tick((dq, ahead, back_moving, do_t), r_o)
        ahead_moving = shift_ctx(ahead, 1)
        dq, own = attend_back(0, dq)
        dq, own, back_moving = tick((dq, own, back_moving), r_gu, r_o)
        dq_t = rotate_t(dq * head_width**-0.5, cosine, -sine, head_width).astype(bf16)
        both_q = plan.halves(h1x, dq_t)
        zr_mlp = plan.reduce_ctx(r_gu.finish() + r_o.finish())
        own, both_q, ahead_moving, dq_t = tick((own, both_q, ahead_moving, dq_t))
        d_kv = own.astype(f32) + back_moving.astype(f32) + ahead_moving.astype(f32)
    else:
        parts = {}
        for offset in sorted(offsets, key=lambda o: -abs(o)):
            dq, parts[offset] = attend_back(offset, dq)
        d_kv = Job(reduce_ring_steps(parts)).finish()
        dq_t = rotate_t(dq * head_width**-0.5, cosine, -sine, head_width).astype(bf16)
        both_q = plan.halves(h1x, dq_t)
        zr_mlp = plan.reduce_ctx(r_gu.finish() + r_o.finish())
    dk_t = rotate_t(d_kv[0], cosine, -sine, head_width).astype(bf16)
    dv_t = d_kv[1].astype(bf16)
    both_k = plan.halves(h1x, dk_t)
    both_v = plan.halves(h1y, dv_t)
    r_qkv = plan.reduce_dp((*both_k, "x"), (*both_v, "y"), (*both_q, "x"))
    dh1x = dot_nn(w_q, dq_t)
    dh1y = dot_nn(w_kv, jnp.concatenate([dk_t, dv_t]))
    dh1x, dh1y = tick((dh1x, dh1y), r_qkv)
    grad_tokens, grad_gain_attn = norm_back_call(
        abs_at, [(dh1x, 0), (dh1y, 1)], x_t, inverse_attn, gain_attn, [(dx, bf16)]
    )
    small_job = plan.sum_all(jnp.stack([grad_gain_attn, grad_gain_mlp, grad_router]))
    (grad_tokens,) = tick((grad_tokens,), r_qkv, zr_mlp, small_job)
    grad_tokens = grad_tokens.T
    (grad_tokens,) = tick((grad_tokens,), r_qkv, small_job)
    zr_qkv = plan.reduce_ctx(r_qkv.finish())
    (grad_tokens,) = tick((grad_tokens,), zr_qkv, zr_mlp, small_job)
    (grad_down,) = zr_d.finish()
    grad_gate, grad_up, grad_out = zr_mlp.finish()
    grad_tokens, grad_down, grad_gate, grad_up, grad_out = tick(
        (grad_tokens, grad_down, grad_gate, grad_up, grad_out), zr_qkv, small_job
    )
    grad_key, grad_value, grad_query = zr_qkv.finish()
    small = small_job.finish()
    return (
        result[None],
        grad_tokens[None],
        grad_query,
        grad_key,
        grad_value,
        grad_out,
        grad_gate,
        grad_up,
        grad_down,
        small[0],
        small[1],
        small[2],
    )


def solution(mesh):
    rows = P("dp", "ctx", None)
    flat = P(("dp", "ctx"))
    return jax.shard_map(
        per_device,
        mesh=mesh,
        in_specs=(rows, rows, P("dp"), P("dp", "ctx"), P()) + (flat,) * 7 + (P(),) * 3,
        out_specs=(rows, rows) + (flat,) * 7 + (P(),) * 3,
        check_vma=False,
    )
```

```python
import functools

import jax
import jax.numpy as jnp
from jax import lax
from jax.experimental import pallas as pl
from jax.experimental.layout import Layout, with_layout_constraint
from jax.experimental.pallas import tpu as pltpu
from jax.sharding import PartitionSpec as P

HEADS = 15
KV_HEADS = 5
HEAD_DIM = 64
FF = 2560

norm_eps = 1e-05
rope_base = 100000.0
neg_big = -1e30
f32 = jnp.float32
bf16 = jnp.bfloat16

order_bits = {"x": (0, 2, 4, 6, 1, 3, 5, 7), "y": (0, 4, 2, 6, 1, 5, 3, 7)}
BLOCKS = 8


def dot_nn(left, right):
    return lax.dot_general(left, right, (((1,), (0,)), ((), ())), preferred_element_type=f32)


def dot_tn(left, right):
    return lax.dot_general(left, right, (((0,), (0,)), ((), ())), preferred_element_type=f32)


def dot_nt(left, right):
    return lax.dot_general(left, right, (((1,), (1,)), ((), ())), preferred_element_type=f32)


def attend_body(first, last, places, head_width, group_size, block, sc, *refs):
    pieces = len(places)
    q_ref = refs[0]
    kv_refs = refs[1 : 1 + pieces]
    at = 1 + pieces
    if not first:
        m_in, l_in, acc_in = refs[at : at + 3]
        at += 3
    if last:
        o_ref, lse_ref = refs[at : at + 2]
        at += 2
        m_ref, l_ref, acc_ref = refs[at : at + 3]
    else:
        m_out, l_out, acc_out = refs[at : at + 3]
        m_ref, l_ref, acc_ref = m_out.at[0], l_out.at[0], acc_out.at[0]
    length = sc[0]
    width = group_size * block
    for qb in range(2):
        q_blk = sc[1 + qb]
        cols = slice(qb * block, (qb + 1) * block)
        q_cat = jnp.concatenate(
            [q_ref[h * head_width : (h + 1) * head_width, cols] for h in range(group_size)], axis=1
        )
        if first:
            m_ref[qb : qb + 1, :] = jnp.full((1, width), neg_big, f32)
            l_ref[qb : qb + 1, :] = jnp.zeros((1, width), f32)
            acc_ref[qb] = jnp.zeros((head_width, width), f32)
        else:
            m_ref[qb : qb + 1, :] = m_in[0, qb : qb + 1, :]
            l_ref[qb : qb + 1, :] = l_in[0, qb : qb + 1, :]
            acc_ref[qb] = acc_in[0, qb]
        for piece in range(pieces):
            for sub in range(2):
                k_blk = sc[1 + 2 * places[piece] + sub]
                start = k_blk * block
                keys = slice(sub * block, (sub + 1) * block)

                def step(masked, piece=piece, keys=keys, k_blk=k_blk, start=start):
                    key_t = kv_refs[piece][0, :, keys]
                    val_t = kv_refs[piece][1, :, keys]
                    scores = dot_tn(key_t, q_cat)
                    if masked:
                        k_pos = start + lax.broadcasted_iota(jnp.int32, (block, block), 0)
                        q_pos = q_blk * block + lax.broadcasted_iota(jnp.int32, (block, block), 1)
                        seen = (k_pos <= q_pos) & (k_pos < length)
                        scores = jnp.concatenate(
                            [
                                jnp.where(seen, scores[:, h * block : (h + 1) * block], neg_big)
                                for h in range(group_size)
                            ],
                            axis=1,
                        )
                    m_old = m_ref[qb : qb + 1, :]
                    m_new = jnp.maximum(m_old, jnp.max(scores, axis=0, keepdims=True))
                    probs = jnp.exp(scores - m_new)
                    alpha = jnp.exp(m_old - m_new)
                    m_ref[qb : qb + 1, :] = m_new
                    l_ref[qb : qb + 1, :] = alpha * l_ref[qb : qb + 1, :] + jnp.sum(
                        probs, axis=0, keepdims=True
                    )
                    acc_ref[qb] = acc_ref[qb] * alpha + dot_nn(val_t, probs.astype(bf16))

                live = (k_blk <= q_blk) & (start < length)
                plain = (k_blk < q_blk) & (start + block <= length)
                pl.when(plain)(functools.partial(step, False))
                pl.when(live & jnp.logical_not(plain))(functools.partial(step, True))
        if last:
            total = l_ref[qb : qb + 1, :]
            out = acc_ref[qb] * (1.0 / total)
            for h in range(group_size):
                o_ref[h * head_width : (h + 1) * head_width, cols] = out[
                    :, h * block : (h + 1) * block
                ].astype(bf16)
            lse_ref[0, qb : qb + 1, :] = m_ref[qb : qb + 1, :] + jnp.log(total)


def attend_call(scalars, places, q_t, pieces, state, last, group_size, head_width):
    rows, tokens = q_t.shape
    kv_count = rows // (group_size * head_width)
    block = tokens // 2
    width = group_size * block
    first = state is None
    q_spec = pl.BlockSpec((group_size * head_width, tokens), lambda g, sc: (g, 0))
    kv_spec = pl.BlockSpec((2, head_width, tokens), lambda g, sc: (0, g, 0))
    row_spec = pl.BlockSpec((1, 2, width), lambda g, sc: (g, 0, 0))
    acc_spec = pl.BlockSpec((1, 2, head_width, width), lambda g, sc: (g, 0, 0, 0))
    row_shape = jax.ShapeDtypeStruct((kv_count, 2, width), f32)
    acc_shape = jax.ShapeDtypeStruct((kv_count, 2, head_width, width), f32)
    in_specs = [q_spec] + [kv_spec] * len(pieces)
    operands = [q_t] + list(pieces)
    aliases = {}
    if not first:
        in_specs += [row_spec, row_spec, acc_spec]
        operands += list(state)
    if last:
        out_specs = [q_spec, row_spec]
        out_shape = [jax.ShapeDtypeStruct((rows, tokens), bf16), row_shape]
        scratch = [
            pltpu.VMEM((2, width), f32),
            pltpu.VMEM((2, width), f32),
            pltpu.VMEM((2, head_width, width), f32),
        ]
    else:
        out_specs = [row_spec, row_spec, acc_spec]
        out_shape = [row_shape, row_shape, acc_shape]
        scratch = []
    body = functools.partial(
        attend_body, first, last, places, head_width, group_size, block
    )
    return pl.pallas_call(
        body,
        grid_spec=pltpu.PrefetchScalarGridSpec(
            num_scalar_prefetch=1,
            grid=(kv_count,),
            in_specs=in_specs,
            out_specs=out_specs,
            scratch_shapes=scratch,
        ),
        out_shape=out_shape,
        input_output_aliases=aliases,
        name="attend_forward",
    )(scalars, *operands)


def attend_back_body(first, places, head_width, group_size, block, sc, *refs):
    pieces = len(places)
    q_ref, do_ref, o_ref, lse_ref = refs[:4]
    kv_refs = refs[4 : 4 + pieces]
    at = 4 + pieces
    if not first:
        dq_in = refs[at]
        at += 1
    dq_ref = refs[at]
    dkv_refs = refs[at + 1 : at + 1 + pieces]
    dkv_acc = refs[at + 1 + pieces]
    length = sc[0]
    dkv_acc[...] = jnp.zeros(dkv_acc.shape, f32)
    if first:
        dq_ref[...] = jnp.zeros(dq_ref.shape, f32)
    else:
        dq_ref[...] = dq_in[...]
    for qb in range(2):
        q_blk = sc[1 + qb]
        cols = slice(qb * block, (qb + 1) * block)

        def side_by_side(ref, cols=cols):
            return jnp.concatenate(
                [ref[h * head_width : (h + 1) * head_width, cols] for h in range(group_size)],
                axis=1,
            )

        q_cat = side_by_side(q_ref)
        do_cat = side_by_side(do_ref)
        o_cat = side_by_side(o_ref)
        delta = jnp.sum(do_cat.astype(f32) * o_cat.astype(f32), axis=0, keepdims=True)
        lse = lse_ref[0, qb : qb + 1, :]
        for piece in range(pieces):
            for sub in range(2):
                k_blk = sc[1 + 2 * places[piece] + sub]
                start = k_blk * block
                keys = slice(sub * block, (sub + 1) * block)

                def step(
                    masked, piece=piece, keys=keys, start=start, q_blk=q_blk, q_cat=q_cat,
                    do_cat=do_cat, delta=delta, lse=lse, cols=cols,
                ):
                    key_t = kv_refs[piece][0, :, keys]
                    val_t = kv_refs[piece][1, :, keys]
                    scores = dot_tn(key_t, q_cat)
                    if masked:
                        k_pos = start + lax.broadcasted_iota(jnp.int32, (block, block), 0)
                        q_pos = q_blk * block + lax.broadcasted_iota(jnp.int32, (block, block), 1)
                        seen = (k_pos <= q_pos) & (k_pos < length)
                        scores = jnp.concatenate(
                            [
                                jnp.where(seen, scores[:, h * block : (h + 1) * block], neg_big)
                                for h in range(group_size)
                            ],
                            axis=1,
                        )
                    probs = jnp.exp(scores - lse)
                    d_probs = dot_tn(val_t, do_cat)
                    d_scores = (probs * (d_probs - delta)).astype(bf16)
                    dkv_acc[piece, 1, :, keys] += dot_nt(do_cat, probs.astype(bf16))
                    dkv_acc[piece, 0, :, keys] += dot_nt(q_cat, d_scores)
                    dq = dot_nn(key_t, d_scores)
                    for h in range(group_size):
                        dq_ref[h * head_width : (h + 1) * head_width, cols] += dq[
                            :, h * block : (h + 1) * block
                        ]

                live = (k_blk <= q_blk) & (start < length)
                plain = (k_blk < q_blk) & (start + block <= length)
                pl.when(plain)(functools.partial(step, False))
                pl.when(live & jnp.logical_not(plain))(functools.partial(step, True))
    for piece in range(pieces):
        dkv_refs[piece][...] = dkv_acc[piece].astype(dkv_refs[piece].dtype)


def attend_back_call(
    scalars, places, q_t, do_t, o_t, lse, pieces, dq_before, types, group_size, head_width
):
    rows, tokens = q_t.shape
    kv_count = rows // (group_size * head_width)
    block = tokens // 2
    width = group_size * block
    first = dq_before is None
    q_spec = pl.BlockSpec((group_size * head_width, tokens), lambda g, sc: (g, 0))
    kv_spec = pl.BlockSpec((2, head_width, tokens), lambda g, sc: (0, g, 0))
    row_spec = pl.BlockSpec((1, 2, width), lambda g, sc: (g, 0, 0))
    in_specs = [q_spec, q_spec, q_spec, row_spec] + [kv_spec] * len(pieces)
    operands = [q_t, do_t, o_t, lse] + list(pieces)
    aliases = {}
    if not first:
        in_specs.append(q_spec)
        operands.append(dq_before)
        aliases = {len(operands): 0}
    body = functools.partial(attend_back_body, first, places, head_width, group_size, block)
    return pl.pallas_call(
        body,
        grid_spec=pltpu.PrefetchScalarGridSpec(
            num_scalar_prefetch=1,
            grid=(kv_count,),
            in_specs=in_specs,
            out_specs=[q_spec] + [kv_spec] * len(pieces),
            scratch_shapes=[pltpu.VMEM((len(pieces), 2, head_width, tokens), f32)],
        ),
        out_shape=[jax.ShapeDtypeStruct((rows, tokens), f32)]
        + [jax.ShapeDtypeStruct(p.shape, t) for p, t in zip(pieces, types)],
        input_output_aliases=aliases,
        name="attend_backward",
    )(scalars, *operands)


def ring_order(size):
    return list(range(0, size, 2)) + list(range(1, size, 2))[::-1]


def ring_member(offset):
    size = lax.axis_size("ctx")
    index = lax.axis_index("ctx")
    place = jnp.where(index % 2 == 0, index // 2, size - 1 - index // 2)
    there = (place + offset) % size
    return jnp.where(2 * there < size, 2 * there, 2 * (size - 1 - there) + 1)


class Move:
    def __init__(self, value, step=None, bit=None):
        self.value, self.step, self.bit = value, step, bit

    def launch(self, value):
        if self.step is None:
            size = lax.axis_size("dp")
            return lax.ppermute(value, "dp", [(i, i ^ self.bit) for i in range(size)])
        order = ring_order(lax.axis_size("ctx"))
        pairs = [(m, order[(i + self.step) % len(order)]) for i, m in enumerate(order)]
        return lax.ppermute(value, "ctx", pairs)


def shift_ctx(value, step):
    return Move(value, step=step)


def swap_dp(value, bit):
    return Move(value, bit=bit)


def is_move(value):
    return isinstance(value, Move)


class Job:
    def __init__(self, steps):
        self.steps = steps
        self.moves = self.pending = self.result = None
        self.done = False
        self.advance(None)
        self.launch(self.operands())

    def advance(self, arrived):
        try:
            self.moves = self.steps.send(arrived)
        except StopIteration as stop:
            self.done, self.moves, self.result = True, [], stop.value

    def operands(self):
        return [m.value for m in jax.tree.leaves(self.moves, is_leaf=is_move)]

    def launch(self, operands):
        leaves, tree = jax.tree.flatten(self.moves, is_leaf=is_move)
        sent = [m.launch(v) for m, v in zip(leaves, operands)]
        self.pending = jax.tree.unflatten(tree, sent)

    def finish(self):
        while not self.done:
            self.advance(self.pending)
            self.launch(self.operands())
        return self.result


def tick(values, *jobs, clock=None):
    live = [job for job in jobs if not job.done]
    if clock is not None:
        values, now = lax.optimization_barrier((values, clock["now"]))
        clock["now"] = now + clock["step"]
    values, arrived, now = lax.optimization_barrier(
        (values, [job.pending for job in live], None if clock is None else clock["now"])
    )
    if clock is not None:
        clock["now"] = now
    for job, got in zip(live, arrived):
        job.advance(got)
        job.launch(job.operands())
    return values


def ring_steps(own, found):
    size = lax.axis_size("ctx")
    found.append((0, own))
    up, down = own, own
    for hop in range(1, size // 2 + 1):
        if hop < size - hop:
            up, down = yield [shift_ctx(up, 1), shift_ctx(down, -1)]
            found += [(-hop, up), (hop, down)]
        else:
            (up,) = yield [shift_ctx(up, 1)]
            found.append((-hop, up))
    return found


def gather_ctx_steps(arrays):
    widths = [a.shape[1] for a in arrays]
    own = jnp.concatenate(arrays, axis=1) if len(arrays) > 1 else arrays[0]
    size = lax.axis_size("ctx")
    found = yield from ring_steps(own, [])
    stack = jnp.zeros((size,) + own.shape, own.dtype)
    for offset, piece in found:
        stack = lax.dynamic_update_index_in_dim(stack, piece, ring_member(offset), 0)
    whole = stack.reshape(size * own.shape[0], own.shape[1])
    cuts = [sum(widths[:i]) for i in range(len(widths) + 1)]
    return [whole[:, lo:hi] for lo, hi in zip(cuts[:-1], cuts[1:])]


def gather_dp_steps(units):
    links = [order_bits[order][1:3] for _, order in units]
    blocks = [block for block, _ in units]
    near = yield [
        [swap_dp(b, early), swap_dp(b, late)] for b, (early, late) in zip(blocks, links)
    ]
    corner = yield [swap_dp(n, late) for (n, _), (_, late) in zip(near, links)]
    kept = [[b, n, f, c] for b, (n, f), c in zip(blocks, near, corner)]
    others = yield [[swap_dp(piece, 1) for piece in pieces] for pieces in kept]
    return [pieces + list(other) for pieces, other in zip(kept, others)]


def reduce_dp_steps(units):
    got = yield [swap_dp(send, 1) for _, send, _ in units]
    stays = [keep for keep, _, _ in units]
    links = [order_bits[order][1:3] for _, _, order in units]
    for level in (1, 0):
        rows = [s.shape[0] // 2 for s in stays]
        goes = [
            (s[r:].astype(f32) + g[r:].astype(f32)).astype(bf16)
            for s, g, r in zip(stays, got, rows)
        ]
        moving = [swap_dp(go, link[level]) for go, link in zip(goes, links)]
        stays = [
            (s[:r].astype(f32) + g[:r].astype(f32)).astype(bf16)
            for s, g, r in zip(stays, got, rows)
        ]
        got = yield moving
    return [(s.astype(f32) + g.astype(f32)).astype(bf16) for s, g in zip(stays, got)]


def reduce_ring_steps(parts):
    size = lax.axis_size("ctx")
    top = size // 2
    total = parts[0].astype(f32)
    up = down = None
    for hop in range(top, 0, -1):
        pieces = [(parts[-hop], up, -1)]
        if hop < size - hop:
            pieces.append((parts[hop], down, 1))
        moving = []
        for piece, carry, step in pieces:
            if carry is not None:
                piece = (piece.astype(f32) + carry.astype(f32)).astype(bf16)
            moving.append(shift_ctx(piece, step))
        got = yield moving
        up = got[0]
        down = got[1] if len(got) > 1 else None
    total = total + up.astype(f32)
    return total if down is None else total + down.astype(f32)


def reduce_ctx_steps(blocks):
    size = lax.axis_size("ctx")
    widths = [b.shape[1] for b in blocks]
    whole = jnp.concatenate(blocks, axis=1) if len(blocks) > 1 else blocks[0]
    stack = whole.reshape(size, whole.shape[0] // size, whole.shape[1])
    parts = {
        offset: lax.dynamic_index_in_dim(stack, ring_member(offset), 0, keepdims=False)
        for offset in range(-(size // 2), (size - 1) // 2 + 1)
    }
    total = yield from reduce_ring_steps(parts)
    cuts = [sum(widths[:i]) for i in range(len(widths) + 1)]
    return [total[:, lo:hi].reshape(-1) for lo, hi in zip(cuts[:-1], cuts[1:])]


def sum_all_steps(value):
    bit = 1
    while bit < lax.axis_size("dp"):
        (got,) = yield [swap_dp(value, bit)]
        value = value + got
        bit *= 2
    up = down = value
    size = lax.axis_size("ctx")
    for hop in range(1, size // 2 + 1):
        if hop < size - hop:
            up, down = yield [shift_ctx(up, 1), shift_ctx(down, -1)]
            value = value + (up + down)
        else:
            (up,) = yield [shift_ctx(up, 1)]
            value = value + up
    return value


LANES = 256


def blocked(value):
    return value.reshape((BLOCKS, value.shape[0] // BLOCKS) + value.shape[1:])


def tile_spec(shape):
    zeros = (0,) * (len(shape) - 1)
    return pl.BlockSpec(tuple(shape[:-1]) + (LANES,), lambda t, index: zeros + (t,))


def whole_spec(shape):
    zeros = (0,) * len(shape)
    return pl.BlockSpec(tuple(shape), lambda t, index: zeros)


def token_call(body, name, index, inputs, outputs, fixed_in=(), fixed_out=()):
    tokens = inputs[0].shape[-1]
    return pl.pallas_call(
        body,
        grid_spec=pltpu.PrefetchScalarGridSpec(
            num_scalar_prefetch=1,
            grid=(tokens // LANES,),
            in_specs=[tile_spec(a.shape) for a in inputs] + [whole_spec(a.shape) for a in fixed_in],
            out_specs=[tile_spec(o.shape) for o in outputs]
            + [whole_spec(o.shape) for o in fixed_out],
        ),
        out_shape=list(outputs) + list(fixed_out),
        name=name,
    )(index, *inputs, *fixed_in)


def norm_body(orders, added, width, index, *refs):
    count = 2 if added else 1
    x_ref = refs[0]
    gain_ref = refs[count]
    outs = refs[count + 1 :]
    inverse_ref = outs[0]
    h_refs = outs[1 : 1 + len(orders)]
    values = x_ref
    total = None
    if added:
        values = outs[1 + len(orders)]
    for i in range(BLOCKS):
        part = x_ref[i].astype(f32)
        if added:
            part = part + refs[1][i]
            values[i] = part
        square = jnp.sum(part * part, axis=0, keepdims=True)
        total = square if total is None else total + square
    inverse = lax.rsqrt(total * (1.0 / width) + norm_eps)
    inverse_ref[...] = inverse
    for at, h_ref in zip(orders, h_refs):
        for i in range(BLOCKS):
            j = index[at * BLOCKS + i]
            h_ref[i] = (values[j].astype(f32) * inverse * gain_ref[j]).astype(bf16)


def norm_call(index, orders, x, added, gain):
    x3 = blocked(x)
    inputs = [x3] + ([blocked(added)] if added is not None else [])
    outputs = [jax.ShapeDtypeStruct((1, x.shape[1]), f32)]
    outputs += [jax.ShapeDtypeStruct(x3.shape, bf16)] * len(orders)
    if added is not None:
        outputs.append(jax.ShapeDtypeStruct(x3.shape, f32))
    body = functools.partial(norm_body, orders, added is not None, x.shape[0])
    got = token_call(body, "norm", index, inputs, outputs, [blocked(gain[:, None])])
    return [got[0]] + [g.reshape(x.shape) for g in got[1:]]


def norm_back_body(at_list, width, extras, index, *refs):
    count = len(at_list)
    grads = refs[:count]
    values, inverse_ref = refs[count : count + 2]
    extra_refs = refs[count + 2 : count + 2 + extras]
    gain_ref = refs[count + 2 + extras]
    outs = refs[count + 3 + extras : count + 3 + 2 * extras]
    sum_ref = refs[count + 3 + 2 * extras]
    inverse = inverse_ref[...]

    def grad_of(i):
        total = None
        for at, ref in zip(at_list, grads):
            part = ref[index[at * BLOCKS + i]]
            total = part if total is None else total + part
        return total

    @pl.when(pl.program_id(0) == 0)
    def _():
        sum_ref[...] = jnp.zeros(sum_ref.shape, f32)

    mean = None
    for i in range(BLOCKS):
        along = grad_of(i) * values[i].astype(f32)
        sum_ref[i] += jnp.sum(along * inverse, axis=1, keepdims=True)
        part = jnp.sum(along * gain_ref[i], axis=0, keepdims=True)
        mean = part if mean is None else mean + part
    factor = mean * (1.0 / width) * (inverse * inverse * inverse)
    for i in range(BLOCKS):
        back = inverse * (grad_of(i) * gain_ref[i]) - values[i].astype(f32) * factor
        for extra, out in zip(extra_refs, outs):
            out[i] = (extra[i] + back).astype(out.dtype)


def norm_back_call(index, grads, values, inverse, gain, extras):
    shape = values.shape
    inputs = [blocked(g) for g, _ in grads] + [blocked(values), inverse]
    inputs += [blocked(e) for e, _ in extras]
    outputs = [jax.ShapeDtypeStruct(blocked(values).shape, t) for _, t in extras]
    column = blocked(gain[:, None])
    body = functools.partial(norm_back_body, [at for _, at in grads], shape[0], len(extras))
    got = token_call(
        body, "norm_back", index, inputs, outputs, [column],
        [jax.ShapeDtypeStruct(column.shape, f32)],
    )
    return [g.reshape(shape) for g in got[:-1]] + [got[-1].reshape(shape[0])]


def pick_body(at, index, in_ref, out_ref):
    for i in range(BLOCKS):
        out_ref[i] = in_ref[index[at * BLOCKS + i]]


def pick_call(index, at, value):
    three = blocked(value)
    (out,) = token_call(
        functools.partial(pick_body, at), "pick", index, [three],
        [jax.ShapeDtypeStruct(three.shape, value.dtype)],
    )
    return out.reshape(value.shape)


def silu_body(parts, index, gate_ref, up_ref, *outs):
    for part in range(parts):
        for i in range(BLOCKS):
            j = index[part * BLOCKS + i]
            gate = gate_ref[j, part]
            outs[part][i] = (gate / (1.0 + jnp.exp(-gate)) * up_ref[j, part]).astype(bf16)


def in_parts(value, parts):
    rows, tokens = value.shape
    return value.reshape(BLOCKS, parts, rows // (BLOCKS * parts), tokens)


def silu_call(index, parts, gate, up):
    rows, tokens = gate.shape
    shape = (BLOCKS, rows // (BLOCKS * parts), tokens)
    got = token_call(
        functools.partial(silu_body, parts), "silu", index,
        [in_parts(gate, parts), in_parts(up, parts)],
        [jax.ShapeDtypeStruct(shape, bf16)] * parts,
    )
    return [g.reshape(rows // parts, tokens) for g in got]


def silu_back_body(parts, index, gate_ref, up_ref, *refs):
    grads, outs = refs[:parts], refs[parts:]
    for part in range(parts):
        for i in range(BLOCKS):
            grad = grads[part][index[part * BLOCKS + i]]
            gate = gate_ref[i, part]
            sigmoid = 1.0 / (1.0 + jnp.exp(-gate))
            slope = sigmoid * (1.0 + gate * (1.0 - sigmoid))
            outs[0][i, part] = (grad * up_ref[i, part] * slope).astype(bf16)
            outs[1][i, part] = (grad * (gate * sigmoid)).astype(bf16)


def silu_back_call(index, gate, up, grads):
    parts = len(grads)
    views = [in_parts(gate, parts), in_parts(up, parts)]
    got = token_call(
        functools.partial(silu_back_body, parts), "silu_back", index,
        views + [blocked(g) for g in grads],
        [jax.ShapeDtypeStruct(views[0].shape, bf16)] * 2,
    )
    return [g.reshape(gate.shape) for g in got]


def rows_of(refs):
    return jnp.concatenate([ref[...] for ref in refs], axis=0)


def even_tile(width, limit):
    tiles = [t for t in range(128, limit + 1, 128) if width % t == 0]
    return tiles[-1] if tiles else width


def product_tn_body(counts, *refs):
    total, at = None, 0
    for count in counts:
        part = dot_tn(rows_of(refs[at : at + count]), refs[at + count][...])
        total = part if total is None else total + part
        at += count + 1
    refs[-1][...] = total


def product_tn(*groups):
    if len(groups[0][0]) == 1:
        return sum(dot_tn(pieces[0], right) for pieces, right in groups)
    width = groups[0][0][0].shape[1]
    tile = even_tile(width, 1280)
    tokens = groups[0][1].shape[1]
    operands, specs = [], []
    for pieces, right in groups:
        operands += [*pieces, right]
        specs += [pl.BlockSpec((pieces[0].shape[0], tile), lambda i: (0, i))] * len(pieces)
        specs.append(pl.BlockSpec(right.shape, lambda i: (0, 0)))
    return pl.pallas_call(
        functools.partial(product_tn_body, [len(pieces) for pieces, _ in groups]),
        grid=(width // tile,),
        in_specs=specs,
        out_specs=pl.BlockSpec((tile, tokens), lambda i: (i, 0)),
        out_shape=jax.ShapeDtypeStruct((width, tokens), f32),
        name="product_tn",
    )(*operands)


def product_nn_body(count, *refs):
    out_ref = refs[-1]
    part = dot_nn(rows_of(refs[:count]), refs[count][...])

    @pl.when(pl.program_id(0) == 0)
    def _():
        out_ref[...] = part.astype(out_ref.dtype)

    @pl.when(pl.program_id(0) > 0)
    def _():
        out_ref[...] += part.astype(out_ref.dtype)


def product_nn(pieces, right, kind=f32):
    if len(pieces) == 1:
        return dot_nn(pieces[0], right).astype(kind)
    rows, width = pieces[0].shape
    tile = even_tile(width, 1280) if kind == f32 else width
    tokens = right.shape[1]
    return pl.pallas_call(
        functools.partial(product_nn_body, len(pieces)),
        grid=(width // tile,),
        in_specs=[pl.BlockSpec((rows, tile), lambda i: (0, i))] * len(pieces)
        + [pl.BlockSpec((tile, tokens), lambda i: (i, 0))],
        out_specs=pl.BlockSpec((rows * len(pieces), tokens), lambda i: (0, 0)),
        out_shape=jax.ShapeDtypeStruct((rows * len(pieces), tokens), kind),
        name="product_nn",
    )(*pieces, right)


def hidden_body(index, *refs):
    gate_w, up_w = refs[:BLOCKS], refs[BLOCKS : 2 * BLOCKS]
    hx_ref, hy_ref, gate_ref, up_ref, first_ref, second_ref = refs[2 * BLOCKS :]
    gate = dot_tn(rows_of(gate_w), hx_ref[...])
    up = dot_tn(rows_of(up_w), hy_ref[...])
    gate_ref[...] = gate
    up_ref[...] = up
    hidden = (gate / (1.0 + jnp.exp(-gate)) * up).astype(bf16)
    rows = hidden.shape[0] // 4
    step = pl.program_id(0)
    for side in range(2):
        core = index[2 * step + side] >> 2
        first_ref[core, 0] = hidden[2 * side * rows : (2 * side + 1) * rows]
        second_ref[core, 0] = hidden[(2 * side + 1) * rows : (2 * side + 2) * rows]


def hidden_call(own_at, abs_at, parts, w_g, w_u, hx, hy):
    if parts == 1:
        gate, up = dot_tn(w_g[0], hx), dot_tn(w_u[0], hy)
        return gate, up, silu_call(own_at, parts, gate, up)
    rows, width = w_g[0].shape
    tokens = hx.shape[1]
    tile = width // 4
    part_rows = width // (2 * BLOCKS)
    w_spec = pl.BlockSpec((rows, tile), lambda i, index: (0, i))
    h_spec = pl.BlockSpec(hx.shape, lambda i, index: (0, 0))
    out_spec = pl.BlockSpec((tile, tokens), lambda i, index: (i, 0))
    part_block = (2, 1, part_rows, tokens)
    part_specs = [
        pl.BlockSpec(part_block, lambda i, index: (0, index[2 * i] & 3, 0, 0)),
        pl.BlockSpec(part_block, lambda i, index: (0, index[BLOCKS + 2 * i] & 3, 0, 0)),
    ]
    gate, up, first, second = pl.pallas_call(
        hidden_body,
        grid_spec=pltpu.PrefetchScalarGridSpec(
            num_scalar_prefetch=1,
            grid=(4,),
            in_specs=[w_spec] * (2 * BLOCKS) + [h_spec] * 2,
            out_specs=[out_spec] * 2 + part_specs,
        ),
        out_shape=[jax.ShapeDtypeStruct((width, tokens), f32)] * 2
        + [jax.ShapeDtypeStruct((2, 4, part_rows, tokens), bf16)] * 2,
        name="hidden",
    )(abs_at, *w_g, *w_u, hx, hy)
    return gate, up, [first.reshape(-1, tokens), second.reshape(-1, tokens)]


def hidden_back_body(parts, index, *refs):
    grad_ref, gate_ref, up_ref = refs[:3]
    weights = refs[3 : 3 + parts * BLOCKS]
    outs = refs[3 + parts * BLOCKS :]
    for part in range(parts):
        grad = dot_nn(rows_of(weights[part * BLOCKS : (part + 1) * BLOCKS]), grad_ref[...])
        rows = grad.shape[0] // BLOCKS
        for i in range(BLOCKS):
            j = index[part * BLOCKS + i]
            piece = grad[i * rows : (i + 1) * rows]
            gate = gate_ref[j, part]
            sigmoid = 1.0 / (1.0 + jnp.exp(-gate))
            slope = sigmoid * (1.0 + gate * (1.0 - sigmoid))
            outs[0][j, part] = (piece * up_ref[j, part] * slope).astype(bf16)
            outs[1][j, part] = (piece * (gate * sigmoid)).astype(bf16)


def hidden_back_call(own_at, abs_at, gate, up, w_d, grad):
    parts = len(w_d)
    if parts == 1:
        return silu_back_call(abs_at, gate, up, [dot_nn(w_d[0][0], grad)])
    views = [in_parts(gate, parts), in_parts(up, parts)]
    got = token_call(
        functools.partial(hidden_back_body, parts), "hidden_back", own_at,
        [grad] + views, [jax.ShapeDtypeStruct(views[0].shape, bf16)] * 2,
        [piece for pieces in w_d for piece in pieces],
    )
    return [g.reshape(gate.shape) for g in got]


def row_major(value):
    return with_layout_constraint(value, Layout(major_to_minor=(0, 1)))


class RowPlan:
    parts = 2

    def indices(self):
        me = lax.axis_index("dp")
        own = me ^ jnp.array(order_bits["x"] + order_bits["y"], jnp.int32)
        at = jnp.arange(2 * BLOCKS, dtype=jnp.int32)
        bits = me ^ (at % BLOCKS)
        in_x = ((bits & 1) << 2) | ((bits >> 1) & 3)
        in_y = ((bits & 1) << 2) | (bits & 2) | ((bits >> 2) & 1)
        return own, jnp.where(at < BLOCKS, in_x, in_y)

    def sum_all(self, value):
        return Job(sum_all_steps(value))

    def gather_ctx(self, arrays):
        return Job(gather_ctx_steps(arrays))

    def gather_dp(self, *units):
        return Job(gather_dp_steps(units))

    def row_parts(self, block):
        rows = block.shape[0] // self.parts
        return [block[i * rows : (i + 1) * rows] for i in range(self.parts)]

    def halves(self, left, right_t):
        half = left.shape[0] // 2
        send = row_major(dot_nt(left[half:], right_t).astype(bf16))
        keep = row_major(dot_nt(left[:half], right_t).astype(bf16))
        return keep, send

    def reduce_dp(self, *units):
        return Job(reduce_dp_steps(units))

    def reduce_ctx(self, blocks):
        return Job(reduce_ctx_steps(blocks))


def at_once(result):
    return result
    yield


class FlatPlan:
    axes = ("dp", "ctx")
    parts = 1

    def indices(self):
        plain = jnp.concatenate([jnp.arange(BLOCKS, dtype=jnp.int32)] * 2)
        return plain, plain

    def sum_all(self, value):
        return Job(at_once(lax.psum(value, self.axes)))

    def gather_ctx(self, arrays):
        return Job(
            at_once(
                [
                    lax.all_gather(a.flat, self.axes, axis=0, tiled=True).reshape(-1, a.width)
                    for a in arrays
                ]
            )
        )

    def gather_dp(self, *units):
        return Job(at_once([[block] for block, _ in units]))

    def row_parts(self, block):
        return [block]

    def halves(self, left, right_t):
        return dot_nt(left, right_t), None

    def reduce_dp(self, *units):
        return Job(at_once([keep for keep, _, _ in units]))

    def reduce_ctx(self, blocks):
        return Job(
            at_once(
                [
                    lax.psum_scatter(b.reshape(-1), self.axes, scatter_dimension=0, tiled=True)
                    for b in blocks
                ]
            )
        )


@jax.tree_util.register_pytree_node_class
class FlatShard:
    def __init__(self, flat, width):
        self.flat, self.width = flat, width

    def tree_flatten(self):
        return (self.flat,), self.width

    @classmethod
    def tree_unflatten(cls, width, leaves):
        return cls(leaves[0], width)


def rotary_t(positions, head_width):
    frequency = rope_base ** (-jnp.arange(0, head_width, 2).astype(f32) / head_width)
    angles = frequency[:, None] * positions.astype(f32)[None, :]
    return jnp.cos(angles), jnp.sin(angles)


def rotate_t(value, cosine, sine, head_width):
    rows, tokens = value.shape
    halves = value.reshape(rows // head_width, 2, head_width // 2, tokens)
    first, second = halves[:, 0], halves[:, 1]
    turned = jnp.stack(
        [first * cosine - second * sine, second * cosine + first * sine], axis=1
    )
    return turned.reshape(rows, tokens)


def per_device(
    tokens,
    cotangent,
    lengths,
    gate_mask,
    block_order,
    w_query,
    w_key,
    w_value,
    w_out,
    w_gate,
    w_up,
    w_down,
    gain_attn,
    gain_mlp,
    w_router,
):
    row_count, model_width = tokens.shape[1:]
    head_width = HEAD_DIM
    group_size = HEADS // KV_HEADS
    kv_width = KV_HEADS * head_width
    q_width = HEADS * head_width
    ctx_size = lax.axis_size("ctx")
    ctx_index = lax.axis_index("ctx")
    shards = (w_query, w_key, w_value, w_out, w_gate, w_up, w_down)
    widths = (q_width, kv_width, kv_width, model_width, FF, FF, model_width)
    by_rows = lax.axis_size("dp") == BLOCKS and all(
        s.shape[0] % w == 0 for s, w in zip(shards, widths)
    )
    plan = RowPlan() if by_rows else FlatPlan()
    wrap = (lambda s, w: s.reshape(-1, w)) if by_rows else FlatShard
    s_q, s_k, s_v = [wrap(s, w) for s, w in zip(shards[:3], widths[:3])]

    z_qkv = plan.gather_ctx([s_k, s_v, s_q])
    later = (tokens, lengths, block_order, gain_attn, gain_mlp) + shards[3:]
    later = tick(later, z_qkv)
    tokens, lengths, block_order, gain_attn, gain_mlp = later[:5]
    s_o, s_g, s_u, s_d = later[5:]
    own_at, abs_at = plan.indices()
    x_t = tokens[0].T
    inverse_attn, h1x, h1y = norm_call(own_at, (0, 1), x_t, None, gain_attn)
    s_g, s_o, h1x, h1y = tick((s_g, s_o, h1x, h1y), z_qkv)
    z_k, z_v, z_q = z_qkv.finish()
    dp_kv = plan.gather_dp((jnp.concatenate([z_k, z_v], axis=1), "y"))
    dp_q = plan.gather_dp((z_q, "x"))
    zj_g = plan.gather_ctx([wrap(s_g, FF)])
    s_u, s_o = tick((s_u, s_o), dp_kv, zj_g)
    block = row_count // 2
    own_rows = 2 * ctx_index + jnp.arange(2, dtype=jnp.int32)
    own_pos = (
        block_order[own_rows][:, None] * block + jnp.arange(block, dtype=jnp.int32)[None, :]
    ).reshape(-1)
    cosine, sine = rotary_t(own_pos, head_width)
    offsets = [0]
    for hop in range(1, ctx_size // 2 + 1):
        offsets += [-hop, hop] if hop < ctx_size - hop else [-hop]
    held = jnp.concatenate(
        [2 * ring_member(o) + jnp.arange(2, dtype=jnp.int32) for o in offsets]
    )
    scalars = jnp.concatenate([lengths.astype(jnp.int32), block_order[held]])
    seq_length = lengths[0]
    s_u, cosine, sine, scalars = tick((s_u, cosine, sine, scalars), dp_kv, dp_q, zj_g)
    (z_g,) = zj_g.finish()
    zj_u = plan.gather_ctx([wrap(s_u, FF)])
    zj_o = plan.gather_ctx([wrap(s_o, model_width)])
    s_d, h1x, h1y, z_g = tick((s_d, h1x, h1y, z_g), dp_kv)
    (w_kv,) = dp_kv.finish()
    kv_raw = product_tn((w_kv, h1y))
    k_t = rotate_t(kv_raw[:kv_width], cosine, sine, head_width)
    kv_own = jnp.stack([k_t, kv_raw[kv_width:]]).astype(bf16)
    h1x, kv_own = tick((h1x, kv_own), dp_q, zj_u, zj_o)
    kv_found = []
    kv_ring = Job(ring_steps(kv_own, kv_found))
    dp_g = plan.gather_dp((z_g, "x"))
    h1x, s_d = tick((h1x, s_d), dp_q)
    (w_q,) = dp_q.finish()
    q_t = rotate_t(product_tn((w_q, h1x)), cosine, sine, head_width).astype(bf16) * bf16(
        head_width**-0.5
    )
    clock = {"now": scalars[:1], "step": jnp.minimum(scalars[:1], 0)}

    def attend(at, pieces, state, last):
        return attend_call(scalars, at, q_t, pieces, state, last, group_size, head_width)

    if by_rows and ctx_size == 4:
        state = attend([0], [kv_own], None, False)
        state, q_t, s_d = tick((state, q_t, s_d), zj_u, zj_o, dp_g, clock=clock)
        dp_o = plan.gather_dp((zj_o.finish()[0], "y"))
        dp_u = plan.gather_dp((zj_u.finish()[0], "y"))
        state, q_t, s_d = tick((state, q_t, s_d), kv_ring, clock=clock)
        state = attend([1, 2], [kv for _, kv in kv_found[1:]], state, False)
        state, q_t, s_d = tick((state, q_t, s_d), kv_ring, dp_o, dp_u, dp_g, clock=clock)
        z_d = plan.gather_ctx([wrap(s_d, model_width)])
        found = kv_ring.finish()
        o_t, lse = attend([3], [found[3][1]], state, True)
        o_t, lse, q_t = tick((o_t, lse, q_t), dp_o, dp_u, dp_g, z_d, clock=clock)
    else:
        dp_u = plan.gather_dp((zj_u.finish()[0], "y"))
        dp_o = plan.gather_dp((zj_o.finish()[0], "y"))
        z_d = plan.gather_ctx([wrap(s_d, model_width)])
        found = kv_ring.finish()
        o_t, lse = attend(list(range(len(found))), [kv for _, kv in found], None, True)
    pieces = [piece for _, piece in found]
    d_orders = ("x", "y")[: plan.parts]
    (w_o,) = dp_o.finish()

    o_rel = pick_call(own_at, 1, o_t)
    attn = product_tn((w_o, o_rel))
    inverse_mlp, h2x, h2y, mid = norm_call(own_at, (0, 1), x_t, attn, gain_mlp)
    h2x, h2y, attn = tick((h2x, h2y, attn), dp_u, z_d)
    (d_block,) = z_d.finish()
    dp_d = plan.gather_dp(*zip(plan.row_parts(d_block), d_orders))
    (w_g,) = dp_g.finish()
    (w_u,) = dp_u.finish()
    gate, up, hidden = hidden_call(own_at, abs_at, plan.parts, w_g, w_u, h2x, h2y)
    gate, up, hidden = tick((gate, up, hidden), dp_d, clock=clock)

    x_f = x_t.astype(f32)
    router = jax.nn.sigmoid(jnp.sum(x_f * w_router[:, None], axis=0, keepdims=True))
    bits = gate_mask.astype(f32)
    chosen = bits * router
    usable = (own_pos < seq_length).astype(f32)[None, :]
    dy = cotangent[0].T.astype(f32) * usable
    db = dy * chosen
    d_mlp = db.astype(bf16)
    both_d = []
    for part in hidden:
        both_d.append(plan.halves(part, d_mlp))
        d_mlp, both_d = tick((d_mlp, both_d), dp_d)
    w_d = dp_d.finish()
    r_d = plan.reduce_dp(*[(*both, o) for both, o in zip(both_d, d_orders)])
    mlp = product_tn(*zip(w_d, hidden))
    d_mlp, mlp = tick((d_mlp, mlp), r_d, clock=clock)
    d_gate, d_up = hidden_back_call(own_at, abs_at, gate, up, w_d, d_mlp)
    d_gate, d_up, mlp = tick((d_gate, d_up, mlp), r_d, clock=clock)
    both_g = plan.halves(h2x, d_gate)
    both_u = plan.halves(h2y, d_up)
    d_gate, d_up, both_g, both_u, mlp = tick((d_gate, d_up, both_g, both_u, mlp), r_d)
    r_gu = plan.reduce_dp((*both_g, "x"), (*both_u, "y"))
    dh2x = product_nn(w_g, d_gate)
    dh2y = product_nn(w_u, d_up)
    branch = attn + mlp
    result = (x_f + chosen * branch).astype(bf16).T
    d_logit = bits * jnp.sum(dy * branch, axis=0, keepdims=True) * router * (1.0 - router)
    grad_router = jnp.sum(d_logit * x_f, axis=1)
    dx = dy + d_logit * w_router[:, None]
    dh2x, dh2y, dx, result, grad_router = tick((dh2x, dh2y, dx, result, grad_router), r_gu)
    d_blocks = r_d.finish()
    zr_d = plan.reduce_ctx([jnp.concatenate(d_blocks) if len(d_blocks) > 1 else d_blocks[0]])
    dx, d_attn, grad_gain_mlp = norm_back_call(
        abs_at, [(dh2x, 0), (dh2y, 1)], mid, inverse_mlp, gain_mlp, [(dx, f32), (db, bf16)]
    )
    do_t = pick_call(abs_at, 1, product_nn(w_o, d_attn, bf16))
    both_o = plan.halves(o_rel, d_attn)
    do_t, both_o, dx, grad_gain_mlp = tick((do_t, both_o, dx, grad_gain_mlp), zr_d)
    r_o = plan.reduce_dp((*both_o, "y"))

    def attend_back(offset, dq):
        dq, part = attend_back_call(
            scalars,
            [offsets.index(offset)],
            q_t,
            do_t,
            o_t,
            lse,
            [pieces[offsets.index(offset)]],
            dq,
            [bf16 if offset else f32],
            group_size,
            head_width,
        )
        return dq, part

    def turn_back(d_kv):
        dk_t = rotate_t(d_kv[0], cosine, -sine, head_width).astype(bf16)
        return dk_t, d_kv[1].astype(bf16)

    dq = None
    if by_rows and ctx_size == 4:
        dq, far = attend_back(-2, None)
        dq, far, do_t, dx = tick((dq, far, do_t, dx), zr_d, r_o, clock=clock)
        far_moving = shift_ctx(far, -1).launch(far)
        dq, back = attend_back(-1, dq)
        dq, back, far_moving, do_t = tick((dq, back, far_moving, do_t), r_gu, clock=clock)
        back = (back.astype(f32) + far_moving.astype(f32)).astype(bf16)
        back_moving = shift_ctx(back, -1).launch(back)
        dq, ahead = attend_back(1, dq)
        dq, ahead, back_moving, do_t = tick(
            (dq, ahead, back_moving, do_t), r_o, clock=clock
        )
        ahead_moving = shift_ctx(ahead, 1).launch(ahead)
        dq, own = attend_back(0, dq)
        dq, own, ahead_moving = tick((dq, own, ahead_moving), r_gu, r_o)
        dq_t = rotate_t(dq * head_width**-0.5, cosine, -sine, head_width).astype(bf16)
        both_q = plan.halves(h1x, dq_t)
        zr_mlp = plan.reduce_ctx(r_gu.finish() + r_o.finish())
        d_kv = own.astype(f32) + back_moving.astype(f32) + ahead_moving.astype(f32)
    else:
        parts = {}
        for offset in sorted(offsets, key=lambda o: -abs(o)):
            dq, parts[offset] = attend_back(offset, dq)
        d_kv = Job(reduce_ring_steps(parts)).finish()
        dq_t = rotate_t(dq * head_width**-0.5, cosine, -sine, head_width).astype(bf16)
        both_q = plan.halves(h1x, dq_t)
        zr_mlp = plan.reduce_ctx(r_gu.finish() + r_o.finish())
    dk_t, dv_t = turn_back(d_kv)
    both_k = plan.halves(h1x, dk_t)
    both_v = plan.halves(h1y, dv_t)
    r_qkv = plan.reduce_dp((*both_k, "x"), (*both_v, "y"), (*both_q, "x"))
    dh1x = product_nn(w_q, dq_t)
    dh1y = product_nn(w_kv, jnp.concatenate([dk_t, dv_t]))
    dh1x, dh1y = tick((dh1x, dh1y), r_qkv)
    grad_tokens, grad_gain_attn = norm_back_call(
        abs_at, [(dh1x, 0), (dh1y, 1)], x_t, inverse_attn, gain_attn, [(dx, bf16)]
    )
    small_job = plan.sum_all(jnp.stack([grad_gain_attn, grad_gain_mlp, grad_router]))
    (grad_tokens,) = tick((grad_tokens,), r_qkv, zr_mlp, small_job)
    grad_tokens = grad_tokens.T
    (grad_tokens,) = tick((grad_tokens,), r_qkv, small_job)
    zr_qkv = plan.reduce_ctx(r_qkv.finish())
    (grad_tokens,) = tick((grad_tokens,), zr_qkv, zr_mlp, small_job)
    (grad_down,) = zr_d.finish()
    grad_gate, grad_up, grad_out = zr_mlp.finish()
    grad_tokens, grad_down, grad_gate, grad_up, grad_out = tick(
        (grad_tokens, grad_down, grad_gate, grad_up, grad_out), zr_qkv, small_job
    )
    grad_key, grad_value, grad_query = zr_qkv.finish()
    small = small_job.finish()
    return (
        result[None],
        grad_tokens[None],
        grad_query,
        grad_key,
        grad_value,
        grad_out,
        grad_gate,
        grad_up,
        grad_down,
        small[0],
        small[1],
        small[2],
    )


def solution(mesh):
    rows = P("dp", "ctx", None)
    flat = P(("dp", "ctx"))
    return jax.shard_map(
        per_device,
        mesh=mesh,
        in_specs=(rows, rows, P("dp"), P("dp", "ctx"), P()) + (flat,) * 7 + (P(),) * 3,
        out_specs=(rows, rows) + (flat,) * 7 + (P(),) * 3,
        check_vma=False,
    )
```

```python
import functools

import jax
import jax.numpy as jnp
from jax import lax
from jax.experimental import pallas as pl
from jax.experimental.layout import Layout, with_layout_constraint
from jax.experimental.pallas import tpu as pltpu
from jax.sharding import PartitionSpec as P

HEADS = 15
KV_HEADS = 5
HEAD_DIM = 64
FF = 2560

norm_eps = 1e-05
rope_base = 100000.0
neg_big = -1e30
f32 = jnp.float32
bf16 = jnp.bfloat16

order_bits = {"x": (0, 2, 4, 6, 1, 3, 5, 7), "y": (0, 4, 2, 6, 1, 5, 3, 7)}
BLOCKS = 8


def dot_nn(left, right):
    return lax.dot_general(left, right, (((1,), (0,)), ((), ())), preferred_element_type=f32)


def dot_tn(left, right):
    return lax.dot_general(left, right, (((0,), (0,)), ((), ())), preferred_element_type=f32)


def dot_nt(left, right):
    return lax.dot_general(left, right, (((1,), (1,)), ((), ())), preferred_element_type=f32)


def attend_body(first, last, places, head_width, group_size, block, sc, *refs):
    pieces = len(places)
    q_ref = refs[0]
    kv_refs = refs[1 : 1 + pieces]
    at = 1 + pieces
    if not first:
        m_in, l_in, acc_in = refs[at : at + 3]
        at += 3
    if last:
        o_ref, lse_ref = refs[at : at + 2]
        at += 2
        m_ref, l_ref, acc_ref = refs[at : at + 3]
    else:
        m_out, l_out, acc_out = refs[at : at + 3]
        m_ref, l_ref, acc_ref = m_out.at[0], l_out.at[0], acc_out.at[0]
    length = sc[0]
    width = group_size * block
    for qb in range(2):
        q_blk = sc[1 + qb]
        cols = slice(qb * block, (qb + 1) * block)
        q_cat = jnp.concatenate(
            [q_ref[h * head_width : (h + 1) * head_width, cols] for h in range(group_size)], axis=1
        )
        if first:
            m_ref[qb : qb + 1, :] = jnp.full((1, width), neg_big, f32)
            l_ref[qb : qb + 1, :] = jnp.zeros((1, width), f32)
            acc_ref[qb] = jnp.zeros((head_width, width), f32)
        else:
            m_ref[qb : qb + 1, :] = m_in[0, qb : qb + 1, :]
            l_ref[qb : qb + 1, :] = l_in[0, qb : qb + 1, :]
            acc_ref[qb] = acc_in[0, qb]
        for piece in range(pieces):
            for sub in range(2):
                k_blk = sc[1 + 2 * places[piece] + sub]
                start = k_blk * block
                keys = slice(sub * block, (sub + 1) * block)

                def step(masked, piece=piece, keys=keys, k_blk=k_blk, start=start):
                    key_t = kv_refs[piece][0, :, keys]
                    val_t = kv_refs[piece][1, :, keys]
                    scores = dot_tn(key_t, q_cat)
                    if masked:
                        k_pos = start + lax.broadcasted_iota(jnp.int32, (block, block), 0)
                        q_pos = q_blk * block + lax.broadcasted_iota(jnp.int32, (block, block), 1)
                        seen = (k_pos <= q_pos) & (k_pos < length)
                        scores = jnp.concatenate(
                            [
                                jnp.where(seen, scores[:, h * block : (h + 1) * block], neg_big)
                                for h in range(group_size)
                            ],
                            axis=1,
                        )
                    m_old = m_ref[qb : qb + 1, :]
                    m_new = jnp.maximum(m_old, jnp.max(scores, axis=0, keepdims=True))
                    probs = jnp.exp(scores - m_new)
                    alpha = jnp.exp(m_old - m_new)
                    m_ref[qb : qb + 1, :] = m_new
                    l_ref[qb : qb + 1, :] = alpha * l_ref[qb : qb + 1, :] + jnp.sum(
                        probs, axis=0, keepdims=True
                    )
                    acc_ref[qb] = acc_ref[qb] * alpha + dot_nn(val_t, probs.astype(bf16))

                live = (k_blk <= q_blk) & (start < length)
                plain = (k_blk < q_blk) & (start + block <= length)
                pl.when(plain)(functools.partial(step, False))
                pl.when(live & jnp.logical_not(plain))(functools.partial(step, True))
        if last:
            total = l_ref[qb : qb + 1, :]
            out = acc_ref[qb] * (1.0 / total)
            for h in range(group_size):
                o_ref[h * head_width : (h + 1) * head_width, cols] = out[
                    :, h * block : (h + 1) * block
                ].astype(bf16)
            lse_ref[0, qb : qb + 1, :] = m_ref[qb : qb + 1, :] + jnp.log(total)


def attend_call(scalars, places, q_t, pieces, state, last, group_size, head_width):
    rows, tokens = q_t.shape
    kv_count = rows // (group_size * head_width)
    block = tokens // 2
    width = group_size * block
    first = state is None
    q_spec = pl.BlockSpec((group_size * head_width, tokens), lambda g, sc: (g, 0))
    kv_spec = pl.BlockSpec((2, head_width, tokens), lambda g, sc: (0, g, 0))
    row_spec = pl.BlockSpec((1, 2, width), lambda g, sc: (g, 0, 0))
    acc_spec = pl.BlockSpec((1, 2, head_width, width), lambda g, sc: (g, 0, 0, 0))
    row_shape = jax.ShapeDtypeStruct((kv_count, 2, width), f32)
    acc_shape = jax.ShapeDtypeStruct((kv_count, 2, head_width, width), f32)
    in_specs = [q_spec] + [kv_spec] * len(pieces)
    operands = [q_t] + list(pieces)
    aliases = {}
    if not first:
        in_specs += [row_spec, row_spec, acc_spec]
        operands += list(state)
    if last:
        out_specs = [q_spec, row_spec]
        out_shape = [jax.ShapeDtypeStruct((rows, tokens), bf16), row_shape]
        scratch = [
            pltpu.VMEM((2, width), f32),
            pltpu.VMEM((2, width), f32),
            pltpu.VMEM((2, head_width, width), f32),
        ]
    else:
        out_specs = [row_spec, row_spec, acc_spec]
        out_shape = [row_shape, row_shape, acc_shape]
        scratch = []
    body = functools.partial(
        attend_body, first, last, places, head_width, group_size, block
    )
    return pl.pallas_call(
        body,
        grid_spec=pltpu.PrefetchScalarGridSpec(
            num_scalar_prefetch=1,
            grid=(kv_count,),
            in_specs=in_specs,
            out_specs=out_specs,
            scratch_shapes=scratch,
        ),
        out_shape=out_shape,
        input_output_aliases=aliases,
        name="attend_forward",
    )(scalars, *operands)


def attend_back_body(first, places, head_width, group_size, block, sc, *refs):
    pieces = len(places)
    q_ref, do_ref, o_ref, lse_ref = refs[:4]
    kv_refs = refs[4 : 4 + pieces]
    at = 4 + pieces
    if not first:
        dq_in = refs[at]
        at += 1
    dq_ref = refs[at]
    dkv_refs = refs[at + 1 : at + 1 + pieces]
    dkv_acc = refs[at + 1 + pieces]
    length = sc[0]
    dkv_acc[...] = jnp.zeros(dkv_acc.shape, f32)
    if first:
        dq_ref[...] = jnp.zeros(dq_ref.shape, f32)
    else:
        dq_ref[...] = dq_in[...]
    for qb in range(2):
        q_blk = sc[1 + qb]
        cols = slice(qb * block, (qb + 1) * block)

        def side_by_side(ref, cols=cols):
            return jnp.concatenate(
                [ref[h * head_width : (h + 1) * head_width, cols] for h in range(group_size)],
                axis=1,
            )

        q_cat = side_by_side(q_ref)
        do_cat = side_by_side(do_ref)
        o_cat = side_by_side(o_ref)
        delta = jnp.sum(do_cat.astype(f32) * o_cat.astype(f32), axis=0, keepdims=True)
        lse = lse_ref[0, qb : qb + 1, :]
        for piece in range(pieces):
            for sub in range(2):
                k_blk = sc[1 + 2 * places[piece] + sub]
                start = k_blk * block
                keys = slice(sub * block, (sub + 1) * block)

                def step(
                    masked, piece=piece, keys=keys, start=start, q_blk=q_blk, q_cat=q_cat,
                    do_cat=do_cat, delta=delta, lse=lse, cols=cols,
                ):
                    key_t = kv_refs[piece][0, :, keys]
                    val_t = kv_refs[piece][1, :, keys]
                    scores = dot_tn(key_t, q_cat)
                    if masked:
                        k_pos = start + lax.broadcasted_iota(jnp.int32, (block, block), 0)
                        q_pos = q_blk * block + lax.broadcasted_iota(jnp.int32, (block, block), 1)
                        seen = (k_pos <= q_pos) & (k_pos < length)
                        scores = jnp.concatenate(
                            [
                                jnp.where(seen, scores[:, h * block : (h + 1) * block], neg_big)
                                for h in range(group_size)
                            ],
                            axis=1,
                        )
                    probs = jnp.exp(scores - lse)
                    d_probs = dot_tn(val_t, do_cat)
                    d_scores = (probs * (d_probs - delta)).astype(bf16)
                    dkv_acc[piece, 1, :, keys] += dot_nt(do_cat, probs.astype(bf16))
                    dkv_acc[piece, 0, :, keys] += dot_nt(q_cat, d_scores)
                    dq = dot_nn(key_t, d_scores)
                    for h in range(group_size):
                        dq_ref[h * head_width : (h + 1) * head_width, cols] += dq[
                            :, h * block : (h + 1) * block
                        ]

                live = (k_blk <= q_blk) & (start < length)
                plain = (k_blk < q_blk) & (start + block <= length)
                pl.when(plain)(functools.partial(step, False))
                pl.when(live & jnp.logical_not(plain))(functools.partial(step, True))
    for piece in range(pieces):
        dkv_refs[piece][...] = dkv_acc[piece].astype(dkv_refs[piece].dtype)


def attend_back_call(
    scalars, places, q_t, do_t, o_t, lse, pieces, dq_before, types, group_size, head_width
):
    rows, tokens = q_t.shape
    kv_count = rows // (group_size * head_width)
    block = tokens // 2
    width = group_size * block
    first = dq_before is None
    q_spec = pl.BlockSpec((group_size * head_width, tokens), lambda g, sc: (g, 0))
    kv_spec = pl.BlockSpec((2, head_width, tokens), lambda g, sc: (0, g, 0))
    row_spec = pl.BlockSpec((1, 2, width), lambda g, sc: (g, 0, 0))
    in_specs = [q_spec, q_spec, q_spec, row_spec] + [kv_spec] * len(pieces)
    operands = [q_t, do_t, o_t, lse] + list(pieces)
    aliases = {}
    if not first:
        in_specs.append(q_spec)
        operands.append(dq_before)
        aliases = {len(operands): 0}
    body = functools.partial(attend_back_body, first, places, head_width, group_size, block)
    return pl.pallas_call(
        body,
        grid_spec=pltpu.PrefetchScalarGridSpec(
            num_scalar_prefetch=1,
            grid=(kv_count,),
            in_specs=in_specs,
            out_specs=[q_spec] + [kv_spec] * len(pieces),
            scratch_shapes=[pltpu.VMEM((len(pieces), 2, head_width, tokens), f32)],
        ),
        out_shape=[jax.ShapeDtypeStruct((rows, tokens), f32)]
        + [jax.ShapeDtypeStruct(p.shape, t) for p, t in zip(pieces, types)],
        input_output_aliases=aliases,
        name="attend_backward",
    )(scalars, *operands)


def ring_order(size):
    return list(range(0, size, 2)) + list(range(1, size, 2))[::-1]


def ring_member(offset):
    size = lax.axis_size("ctx")
    index = lax.axis_index("ctx")
    place = jnp.where(index % 2 == 0, index // 2, size - 1 - index // 2)
    there = (place + offset) % size
    return jnp.where(2 * there < size, 2 * there, 2 * (size - 1 - there) + 1)


class Move:
    def __init__(self, value, step=None, bit=None):
        self.value, self.step, self.bit = value, step, bit

    def launch(self, value):
        if self.step is None:
            size = lax.axis_size("dp")
            return lax.ppermute(value, "dp", [(i, i ^ self.bit) for i in range(size)])
        order = ring_order(lax.axis_size("ctx"))
        pairs = [(m, order[(i + self.step) % len(order)]) for i, m in enumerate(order)]
        return lax.ppermute(value, "ctx", pairs)


def shift_ctx(value, step):
    return Move(value, step=step)


def swap_dp(value, bit):
    return Move(value, bit=bit)


def is_move(value):
    return isinstance(value, Move)


class Job:
    def __init__(self, steps):
        self.steps = steps
        self.moves = self.pending = self.result = None
        self.done = False
        self.advance(None)
        self.launch(self.operands())

    def advance(self, arrived):
        try:
            self.moves = self.steps.send(arrived)
        except StopIteration as stop:
            self.done, self.moves, self.result = True, [], stop.value

    def operands(self):
        return [m.value for m in jax.tree.leaves(self.moves, is_leaf=is_move)]

    def launch(self, operands):
        leaves, tree = jax.tree.flatten(self.moves, is_leaf=is_move)
        sent = [m.launch(v) for m, v in zip(leaves, operands)]
        self.pending = jax.tree.unflatten(tree, sent)

    def finish(self):
        while not self.done:
            self.advance(self.pending)
            self.launch(self.operands())
        return self.result


def tick(values, *jobs, clock=None):
    live = [job for job in jobs if not job.done]
    if clock is not None:
        values, now = lax.optimization_barrier((values, clock["now"]))
        clock["now"] = now + clock["step"]
    values, arrived, now = lax.optimization_barrier(
        (values, [job.pending for job in live], None if clock is None else clock["now"])
    )
    if clock is not None:
        clock["now"] = now
    for job, got in zip(live, arrived):
        job.advance(got)
        job.launch(job.operands())
    return values


def ring_steps(own, found):
    size = lax.axis_size("ctx")
    found.append((0, own))
    up, down = own, own
    for hop in range(1, size // 2 + 1):
        if hop < size - hop:
            up, down = yield [shift_ctx(up, 1), shift_ctx(down, -1)]
            found += [(-hop, up), (hop, down)]
        else:
            (up,) = yield [shift_ctx(up, 1)]
            found.append((-hop, up))
    return found


def gather_ctx_steps(arrays):
    widths = [a.shape[1] for a in arrays]
    own = jnp.concatenate(arrays, axis=1) if len(arrays) > 1 else arrays[0]
    size = lax.axis_size("ctx")
    found = yield from ring_steps(own, [])
    stack = jnp.zeros((size,) + own.shape, own.dtype)
    for offset, piece in found:
        stack = lax.dynamic_update_index_in_dim(stack, piece, ring_member(offset), 0)
    whole = stack.reshape(size * own.shape[0], own.shape[1])
    cuts = [sum(widths[:i]) for i in range(len(widths) + 1)]
    return [whole[:, lo:hi] for lo, hi in zip(cuts[:-1], cuts[1:])]


def gather_dp_steps(units):
    links = [order_bits[order][1:3] for _, order in units]
    blocks = [block for block, _ in units]
    near = yield [
        [swap_dp(b, early), swap_dp(b, late)] for b, (early, late) in zip(blocks, links)
    ]
    corner = yield [swap_dp(n, late) for (n, _), (_, late) in zip(near, links)]
    kept = [[b, n, f, c] for b, (n, f), c in zip(blocks, near, corner)]
    others = yield [[swap_dp(piece, 1) for piece in pieces] for pieces in kept]
    return [pieces + list(other) for pieces, other in zip(kept, others)]


def reduce_dp_steps(units):
    got = yield [swap_dp(send, 1) for _, send, _ in units]
    stays = [keep for keep, _, _ in units]
    links = [order_bits[order][1:3] for _, _, order in units]
    for level in (1, 0):
        rows = [s.shape[0] // 2 for s in stays]
        goes = [
            (s[r:].astype(f32) + g[r:].astype(f32)).astype(bf16)
            for s, g, r in zip(stays, got, rows)
        ]
        moving = [swap_dp(go, link[level]) for go, link in zip(goes, links)]
        stays = [
            (s[:r].astype(f32) + g[:r].astype(f32)).astype(bf16)
            for s, g, r in zip(stays, got, rows)
        ]
        got = yield moving
    return [(s.astype(f32) + g.astype(f32)).astype(bf16) for s, g in zip(stays, got)]


def reduce_ring_steps(parts):
    size = lax.axis_size("ctx")
    top = size // 2
    total = parts[0].astype(f32)
    up = down = None
    for hop in range(top, 0, -1):
        pieces = [(parts[-hop], up, -1)]
        if hop < size - hop:
            pieces.append((parts[hop], down, 1))
        moving = []
        for piece, carry, step in pieces:
            if carry is not None:
                piece = (piece.astype(f32) + carry.astype(f32)).astype(bf16)
            moving.append(shift_ctx(piece, step))
        got = yield moving
        up = got[0]
        down = got[1] if len(got) > 1 else None
    total = total + up.astype(f32)
    return total if down is None else total + down.astype(f32)


def reduce_ctx_steps(blocks):
    size = lax.axis_size("ctx")
    widths = [b.shape[1] for b in blocks]
    whole = jnp.concatenate(blocks, axis=1) if len(blocks) > 1 else blocks[0]
    stack = whole.reshape(size, whole.shape[0] // size, whole.shape[1])
    parts = {
        offset: lax.dynamic_index_in_dim(stack, ring_member(offset), 0, keepdims=False)
        for offset in range(-(size // 2), (size - 1) // 2 + 1)
    }
    total = yield from reduce_ring_steps(parts)
    cuts = [sum(widths[:i]) for i in range(len(widths) + 1)]
    return [total[:, lo:hi].reshape(-1) for lo, hi in zip(cuts[:-1], cuts[1:])]


def sum_all_steps(value):
    bit = 1
    while bit < lax.axis_size("dp"):
        (got,) = yield [swap_dp(value, bit)]
        value = value + got
        bit *= 2
    up = down = value
    size = lax.axis_size("ctx")
    for hop in range(1, size // 2 + 1):
        if hop < size - hop:
            up, down = yield [shift_ctx(up, 1), shift_ctx(down, -1)]
            value = value + (up + down)
        else:
            (up,) = yield [shift_ctx(up, 1)]
            value = value + up
    return value


LANES = 256


def blocked(value):
    return value.reshape((BLOCKS, value.shape[0] // BLOCKS) + value.shape[1:])


def tile_spec(shape):
    zeros = (0,) * (len(shape) - 1)
    return pl.BlockSpec(tuple(shape[:-1]) + (LANES,), lambda t, index: zeros + (t,))


def whole_spec(shape):
    zeros = (0,) * len(shape)
    return pl.BlockSpec(tuple(shape), lambda t, index: zeros)


def token_call(body, name, index, inputs, outputs, fixed_in=(), fixed_out=()):
    tokens = inputs[0].shape[-1]
    return pl.pallas_call(
        body,
        grid_spec=pltpu.PrefetchScalarGridSpec(
            num_scalar_prefetch=1,
            grid=(tokens // LANES,),
            in_specs=[tile_spec(a.shape) for a in inputs] + [whole_spec(a.shape) for a in fixed_in],
            out_specs=[tile_spec(o.shape) for o in outputs]
            + [whole_spec(o.shape) for o in fixed_out],
        ),
        out_shape=list(outputs) + list(fixed_out),
        name=name,
    )(index, *inputs, *fixed_in)


def norm_body(orders, added, width, index, *refs):
    count = 2 if added else 1
    x_ref = refs[0]
    gain_ref = refs[count]
    outs = refs[count + 1 :]
    inverse_ref = outs[0]
    h_refs = outs[1 : 1 + len(orders)]
    values = x_ref
    total = None
    if added:
        values = outs[1 + len(orders)]
    for i in range(BLOCKS):
        part = x_ref[i].astype(f32)
        if added:
            part = part + refs[1][i]
            values[i] = part
        square = jnp.sum(part * part, axis=0, keepdims=True)
        total = square if total is None else total + square
    inverse = lax.rsqrt(total * (1.0 / width) + norm_eps)
    inverse_ref[...] = inverse
    for at, h_ref in zip(orders, h_refs):
        for i in range(BLOCKS):
            j = index[at * BLOCKS + i]
            h_ref[i] = (values[j].astype(f32) * inverse * gain_ref[j]).astype(bf16)


def norm_call(index, orders, x, added, gain):
    x3 = blocked(x)
    inputs = [x3] + ([blocked(added)] if added is not None else [])
    outputs = [jax.ShapeDtypeStruct((1, x.shape[1]), f32)]
    outputs += [jax.ShapeDtypeStruct(x3.shape, bf16)] * len(orders)
    if added is not None:
        outputs.append(jax.ShapeDtypeStruct(x3.shape, f32))
    body = functools.partial(norm_body, orders, added is not None, x.shape[0])
    got = token_call(body, "norm", index, inputs, outputs, [blocked(gain[:, None])])
    return [got[0]] + [g.reshape(x.shape) for g in got[1:]]


def norm_back_body(at_list, width, extras, index, *refs):
    count = len(at_list)
    grads = refs[:count]
    values, inverse_ref = refs[count : count + 2]
    extra_refs = refs[count + 2 : count + 2 + extras]
    gain_ref = refs[count + 2 + extras]
    outs = refs[count + 3 + extras : count + 3 + 2 * extras]
    sum_ref = refs[count + 3 + 2 * extras]
    inverse = inverse_ref[...]

    def grad_of(i):
        total = None
        for at, ref in zip(at_list, grads):
            part = ref[index[at * BLOCKS + i]]
            total = part if total is None else total + part
        return total

    @pl.when(pl.program_id(0) == 0)
    def _():
        sum_ref[...] = jnp.zeros(sum_ref.shape, f32)

    mean = None
    for i in range(BLOCKS):
        along = grad_of(i) * values[i].astype(f32)
        sum_ref[i] += jnp.sum(along * inverse, axis=1, keepdims=True)
        part = jnp.sum(along * gain_ref[i], axis=0, keepdims=True)
        mean = part if mean is None else mean + part
    factor = mean * (1.0 / width) * (inverse * inverse * inverse)
    for i in range(BLOCKS):
        back = inverse * (grad_of(i) * gain_ref[i]) - values[i].astype(f32) * factor
        for extra, out in zip(extra_refs, outs):
            out[i] = (extra[i] + back).astype(out.dtype)


def norm_back_call(index, grads, values, inverse, gain, extras):
    shape = values.shape
    inputs = [blocked(g) for g, _ in grads] + [blocked(values), inverse]
    inputs += [blocked(e) for e, _ in extras]
    outputs = [jax.ShapeDtypeStruct(blocked(values).shape, t) for _, t in extras]
    column = blocked(gain[:, None])
    body = functools.partial(norm_back_body, [at for _, at in grads], shape[0], len(extras))
    got = token_call(
        body, "norm_back", index, inputs, outputs, [column],
        [jax.ShapeDtypeStruct(column.shape, f32)],
    )
    return [g.reshape(shape) for g in got[:-1]] + [got[-1].reshape(shape[0])]


def pick_body(at, index, in_ref, out_ref):
    for i in range(BLOCKS):
        out_ref[i] = in_ref[index[at * BLOCKS + i]]


def pick_call(index, at, value):
    three = blocked(value)
    (out,) = token_call(
        functools.partial(pick_body, at), "pick", index, [three],
        [jax.ShapeDtypeStruct(three.shape, value.dtype)],
    )
    return out.reshape(value.shape)


def silu_body(parts, index, gate_ref, up_ref, *outs):
    for part in range(parts):
        for i in range(BLOCKS):
            j = index[part * BLOCKS + i]
            gate = gate_ref[j, part]
            outs[part][i] = (gate / (1.0 + jnp.exp(-gate)) * up_ref[j, part]).astype(bf16)


def in_parts(value, parts):
    rows, tokens = value.shape
    return value.reshape(BLOCKS, parts, rows // (BLOCKS * parts), tokens)


def silu_call(index, parts, gate, up):
    rows, tokens = gate.shape
    shape = (BLOCKS, rows // (BLOCKS * parts), tokens)
    got = token_call(
        functools.partial(silu_body, parts), "silu", index,
        [in_parts(gate, parts), in_parts(up, parts)],
        [jax.ShapeDtypeStruct(shape, bf16)] * parts,
    )
    return [g.reshape(rows // parts, tokens) for g in got]


def silu_back_body(parts, index, gate_ref, up_ref, *refs):
    grads, outs = refs[:parts], refs[parts:]
    for part in range(parts):
        for i in range(BLOCKS):
            grad = grads[part][index[part * BLOCKS + i]]
            gate = gate_ref[i, part]
            sigmoid = 1.0 / (1.0 + jnp.exp(-gate))
            slope = sigmoid * (1.0 + gate * (1.0 - sigmoid))
            outs[0][i, part] = (grad * up_ref[i, part] * slope).astype(bf16)
            outs[1][i, part] = (grad * (gate * sigmoid)).astype(bf16)


def silu_back_call(index, gate, up, grads):
    parts = len(grads)
    views = [in_parts(gate, parts), in_parts(up, parts)]
    got = token_call(
        functools.partial(silu_back_body, parts), "silu_back", index,
        views + [blocked(g) for g in grads],
        [jax.ShapeDtypeStruct(views[0].shape, bf16)] * 2,
    )
    return [g.reshape(gate.shape) for g in got]


def rows_of(refs):
    return jnp.concatenate([ref[...] for ref in refs], axis=0)


def even_tile(width, limit):
    tiles = [t for t in range(128, limit + 1, 128) if width % t == 0]
    return tiles[-1] if tiles else width


def product_tn_body(counts, *refs):
    total, at = None, 0
    for count in counts:
        part = dot_tn(rows_of(refs[at : at + count]), refs[at + count][...])
        total = part if total is None else total + part
        at += count + 1
    refs[-1][...] = total


def product_tn(*groups):
    if len(groups[0][0]) == 1:
        return sum(dot_tn(pieces[0], right) for pieces, right in groups)
    width = groups[0][0][0].shape[1]
    tile = even_tile(width, 1280)
    tokens = groups[0][1].shape[1]
    operands, specs = [], []
    for pieces, right in groups:
        operands += [*pieces, right]
        specs += [pl.BlockSpec((pieces[0].shape[0], tile), lambda i: (0, i))] * len(pieces)
        specs.append(pl.BlockSpec(right.shape, lambda i: (0, 0)))
    return pl.pallas_call(
        functools.partial(product_tn_body, [len(pieces) for pieces, _ in groups]),
        grid=(width // tile,),
        in_specs=specs,
        out_specs=pl.BlockSpec((tile, tokens), lambda i: (i, 0)),
        out_shape=jax.ShapeDtypeStruct((width, tokens), f32),
        name="product_tn",
    )(*operands)


def product_nn_body(count, *refs):
    out_ref = refs[-1]
    part = dot_nn(rows_of(refs[:count]), refs[count][...])

    @pl.when(pl.program_id(0) == 0)
    def _():
        out_ref[...] = part.astype(out_ref.dtype)

    @pl.when(pl.program_id(0) > 0)
    def _():
        out_ref[...] += part.astype(out_ref.dtype)


def product_nn(pieces, right, kind=f32):
    if len(pieces) == 1:
        return dot_nn(pieces[0], right).astype(kind)
    rows, width = pieces[0].shape
    tile = even_tile(width, 1280) if kind == f32 else width
    tokens = right.shape[1]
    return pl.pallas_call(
        functools.partial(product_nn_body, len(pieces)),
        grid=(width // tile,),
        in_specs=[pl.BlockSpec((rows, tile), lambda i: (0, i))] * len(pieces)
        + [pl.BlockSpec((tile, tokens), lambda i: (i, 0))],
        out_specs=pl.BlockSpec((rows * len(pieces), tokens), lambda i: (0, 0)),
        out_shape=jax.ShapeDtypeStruct((rows * len(pieces), tokens), kind),
        name="product_nn",
    )(*pieces, right)


def hidden_body(index, *refs):
    gate_w, up_w = refs[:BLOCKS], refs[BLOCKS : 2 * BLOCKS]
    hx_ref, hy_ref, gate_ref, up_ref, first_ref, second_ref = refs[2 * BLOCKS :]
    gate = dot_tn(rows_of(gate_w), hx_ref[...])
    up = dot_tn(rows_of(up_w), hy_ref[...])
    gate_ref[...] = gate
    up_ref[...] = up
    hidden = (gate / (1.0 + jnp.exp(-gate)) * up).astype(bf16)
    rows = hidden.shape[0] // 4
    step = pl.program_id(0)
    for side in range(2):
        core = index[2 * step + side] >> 2
        first_ref[core, 0] = hidden[2 * side * rows : (2 * side + 1) * rows]
        second_ref[core, 0] = hidden[(2 * side + 1) * rows : (2 * side + 2) * rows]


def hidden_call(own_at, abs_at, parts, w_g, w_u, hx, hy):
    if parts == 1:
        gate, up = dot_tn(w_g[0], hx), dot_tn(w_u[0], hy)
        return gate, up, silu_call(own_at, parts, gate, up)
    rows, width = w_g[0].shape
    tokens = hx.shape[1]
    tile = width // 4
    part_rows = width // (2 * BLOCKS)
    w_spec = pl.BlockSpec((rows, tile), lambda i, index: (0, i))
    h_spec = pl.BlockSpec(hx.shape, lambda i, index: (0, 0))
    out_spec = pl.BlockSpec((tile, tokens), lambda i, index: (i, 0))
    part_block = (2, 1, part_rows, tokens)
    part_specs = [
        pl.BlockSpec(part_block, lambda i, index: (0, index[2 * i] & 3, 0, 0)),
        pl.BlockSpec(part_block, lambda i, index: (0, index[BLOCKS + 2 * i] & 3, 0, 0)),
    ]
    gate, up, first, second = pl.pallas_call(
        hidden_body,
        grid_spec=pltpu.PrefetchScalarGridSpec(
            num_scalar_prefetch=1,
            grid=(4,),
            in_specs=[w_spec] * (2 * BLOCKS) + [h_spec] * 2,
            out_specs=[out_spec] * 2 + part_specs,
        ),
        out_shape=[jax.ShapeDtypeStruct((width, tokens), f32)] * 2
        + [jax.ShapeDtypeStruct((2, 4, part_rows, tokens), bf16)] * 2,
        name="hidden",
    )(abs_at, *w_g, *w_u, hx, hy)
    return gate, up, [first.reshape(-1, tokens), second.reshape(-1, tokens)]


def hidden_back_body(parts, index, *refs):
    grad_ref, gate_ref, up_ref = refs[:3]
    weights = refs[3 : 3 + parts * BLOCKS]
    outs = refs[3 + parts * BLOCKS :]
    for part in range(parts):
        grad = dot_nn(rows_of(weights[part * BLOCKS : (part + 1) * BLOCKS]), grad_ref[...])
        rows = grad.shape[0] // BLOCKS
        for i in range(BLOCKS):
            j = index[part * BLOCKS + i]
            piece = grad[i * rows : (i + 1) * rows]
            gate = gate_ref[j, part]
            sigmoid = 1.0 / (1.0 + jnp.exp(-gate))
            slope = sigmoid * (1.0 + gate * (1.0 - sigmoid))
            outs[0][j, part] = (piece * up_ref[j, part] * slope).astype(bf16)
            outs[1][j, part] = (piece * (gate * sigmoid)).astype(bf16)


def hidden_back_call(own_at, abs_at, gate, up, w_d, grad):
    parts = len(w_d)
    if parts == 1:
        return silu_back_call(abs_at, gate, up, [dot_nn(w_d[0][0], grad)])
    views = [in_parts(gate, parts), in_parts(up, parts)]
    got = token_call(
        functools.partial(hidden_back_body, parts), "hidden_back", own_at,
        [grad] + views, [jax.ShapeDtypeStruct(views[0].shape, bf16)] * 2,
        [piece for pieces in w_d for piece in pieces],
    )
    return [g.reshape(gate.shape) for g in got]


def row_major(value):
    return with_layout_constraint(value, Layout(major_to_minor=(0, 1)))


class RowPlan:
    parts = 2

    def indices(self):
        me = lax.axis_index("dp")
        own = me ^ jnp.array(order_bits["x"] + order_bits["y"], jnp.int32)
        at = jnp.arange(2 * BLOCKS, dtype=jnp.int32)
        bits = me ^ (at % BLOCKS)
        in_x = ((bits & 1) << 2) | ((bits >> 1) & 3)
        in_y = ((bits & 1) << 2) | (bits & 2) | ((bits >> 2) & 1)
        return own, jnp.where(at < BLOCKS, in_x, in_y)

    def sum_all(self, value):
        return Job(sum_all_steps(value))

    def gather_ctx(self, arrays):
        return Job(gather_ctx_steps(arrays))

    def gather_dp(self, *units):
        return Job(gather_dp_steps(units))

    def row_parts(self, block):
        rows = block.shape[0] // self.parts
        return [block[i * rows : (i + 1) * rows] for i in range(self.parts)]

    def halves(self, left, right_t):
        half = left.shape[0] // 2
        send = row_major(dot_nt(left[half:], right_t).astype(bf16))
        keep = row_major(dot_nt(left[:half], right_t).astype(bf16))
        return keep, send

    def reduce_dp(self, *units):
        return Job(reduce_dp_steps(units))

    def reduce_ctx(self, blocks):
        return Job(reduce_ctx_steps(blocks))


def at_once(result):
    return result
    yield


class FlatPlan:
    axes = ("dp", "ctx")
    parts = 1

    def indices(self):
        plain = jnp.concatenate([jnp.arange(BLOCKS, dtype=jnp.int32)] * 2)
        return plain, plain

    def sum_all(self, value):
        return Job(at_once(lax.psum(value, self.axes)))

    def gather_ctx(self, arrays):
        return Job(
            at_once(
                [
                    lax.all_gather(a.flat, self.axes, axis=0, tiled=True).reshape(-1, a.width)
                    for a in arrays
                ]
            )
        )

    def gather_dp(self, *units):
        return Job(at_once([[block] for block, _ in units]))

    def row_parts(self, block):
        return [block]

    def halves(self, left, right_t):
        return dot_nt(left, right_t), None

    def reduce_dp(self, *units):
        return Job(at_once([keep for keep, _, _ in units]))

    def reduce_ctx(self, blocks):
        return Job(
            at_once(
                [
                    lax.psum_scatter(b.reshape(-1), self.axes, scatter_dimension=0, tiled=True)
                    for b in blocks
                ]
            )
        )


@jax.tree_util.register_pytree_node_class
class FlatShard:
    def __init__(self, flat, width):
        self.flat, self.width = flat, width

    def tree_flatten(self):
        return (self.flat,), self.width

    @classmethod
    def tree_unflatten(cls, width, leaves):
        return cls(leaves[0], width)


def rotary_t(positions, head_width):
    frequency = rope_base ** (-jnp.arange(0, head_width, 2).astype(f32) / head_width)
    angles = frequency[:, None] * positions.astype(f32)[None, :]
    return jnp.cos(angles), jnp.sin(angles)


def rotate_t(value, cosine, sine, head_width):
    rows, tokens = value.shape
    halves = value.reshape(rows // head_width, 2, head_width // 2, tokens)
    first, second = halves[:, 0], halves[:, 1]
    turned = jnp.stack(
        [first * cosine - second * sine, second * cosine + first * sine], axis=1
    )
    return turned.reshape(rows, tokens)


def per_device(
    tokens,
    cotangent,
    lengths,
    gate_mask,
    block_order,
    w_query,
    w_key,
    w_value,
    w_out,
    w_gate,
    w_up,
    w_down,
    gain_attn,
    gain_mlp,
    w_router,
):
    row_count, model_width = tokens.shape[1:]
    head_width = HEAD_DIM
    group_size = HEADS // KV_HEADS
    kv_width = KV_HEADS * head_width
    q_width = HEADS * head_width
    ctx_size = lax.axis_size("ctx")
    ctx_index = lax.axis_index("ctx")
    shards = (w_query, w_key, w_value, w_out, w_gate, w_up, w_down)
    widths = (q_width, kv_width, kv_width, model_width, FF, FF, model_width)
    by_rows = lax.axis_size("dp") == BLOCKS and all(
        s.shape[0] % w == 0 for s, w in zip(shards, widths)
    )
    plan = RowPlan() if by_rows else FlatPlan()
    wrap = (lambda s, w: s.reshape(-1, w)) if by_rows else FlatShard
    s_q, s_k, s_v = [wrap(s, w) for s, w in zip(shards[:3], widths[:3])]

    z_qkv = plan.gather_ctx([s_k, s_v, s_q])
    later = (tokens, lengths, block_order, gain_attn, gain_mlp) + shards[3:]
    later = tick(later, z_qkv)
    tokens, lengths, block_order, gain_attn, gain_mlp = later[:5]
    s_o, s_g, s_u, s_d = later[5:]
    own_at, abs_at = plan.indices()
    x_t = tokens[0].T
    inverse_attn, h1x, h1y = norm_call(own_at, (0, 1), x_t, None, gain_attn)
    s_g, s_o, h1x, h1y = tick((s_g, s_o, h1x, h1y), z_qkv)
    z_k, z_v, z_q = z_qkv.finish()
    dp_kv = plan.gather_dp((jnp.concatenate([z_k, z_v], axis=1), "y"))
    dp_q = plan.gather_dp((z_q, "x"))
    zj_g = plan.gather_ctx([wrap(s_g, FF)])
    s_u, s_o = tick((s_u, s_o), dp_kv, zj_g)
    block = row_count // 2
    own_rows = 2 * ctx_index + jnp.arange(2, dtype=jnp.int32)
    own_pos = (
        block_order[own_rows][:, None] * block + jnp.arange(block, dtype=jnp.int32)[None, :]
    ).reshape(-1)
    cosine, sine = rotary_t(own_pos, head_width)
    offsets = [0]
    for hop in range(1, ctx_size // 2 + 1):
        offsets += [-hop, hop] if hop < ctx_size - hop else [-hop]
    held = jnp.concatenate(
        [2 * ring_member(o) + jnp.arange(2, dtype=jnp.int32) for o in offsets]
    )
    scalars = jnp.concatenate([lengths.astype(jnp.int32), block_order[held]])
    seq_length = lengths[0]
    s_u, cosine, sine, scalars = tick((s_u, cosine, sine, scalars), dp_kv, dp_q, zj_g)
    (z_g,) = zj_g.finish()
    zj_u = plan.gather_ctx([wrap(s_u, FF)])
    zj_o = plan.gather_ctx([wrap(s_o, model_width)])
    s_d, h1x, h1y, z_g = tick((s_d, h1x, h1y, z_g), dp_kv)
    (w_kv,) = dp_kv.finish()
    kv_raw = product_tn((w_kv, h1y))
    k_t = rotate_t(kv_raw[:kv_width], cosine, sine, head_width)
    kv_own = jnp.stack([k_t, kv_raw[kv_width:]]).astype(bf16)
    h1x, kv_own = tick((h1x, kv_own), dp_q, zj_u, zj_o)
    kv_found = []
    kv_ring = Job(ring_steps(kv_own, kv_found))
    dp_g = plan.gather_dp((z_g, "x"))
    h1x, s_d = tick((h1x, s_d), dp_q)
    (w_q,) = dp_q.finish()
    q_t = rotate_t(product_tn((w_q, h1x)), cosine, sine, head_width).astype(bf16) * bf16(
        head_width**-0.5
    )
    clock = {"now": scalars[:1], "step": jnp.minimum(scalars[:1], 0)}

    def attend(at, pieces, state, last):
        return attend_call(scalars, at, q_t, pieces, state, last, group_size, head_width)

    if by_rows and ctx_size == 4:
        state = attend([0], [kv_own], None, False)
        state, q_t, s_d = tick((state, q_t, s_d), zj_u, zj_o, dp_g, clock=clock)
        dp_o = plan.gather_dp((zj_o.finish()[0], "y"))
        dp_u = plan.gather_dp((zj_u.finish()[0], "y"))
        state, q_t, s_d = tick((state, q_t, s_d), kv_ring, clock=clock)
        state = attend([1, 2], [kv for _, kv in kv_found[1:]], state, False)
        state, q_t, s_d = tick((state, q_t, s_d), kv_ring, dp_o, dp_u, dp_g, clock=clock)
        z_d = plan.gather_ctx([wrap(s_d, model_width)])
        found = kv_ring.finish()
        o_t, lse = attend([3], [found[3][1]], state, True)
        o_t, lse, q_t = tick((o_t, lse, q_t), dp_o, dp_u, dp_g, z_d, clock=clock)
    else:
        dp_u = plan.gather_dp((zj_u.finish()[0], "y"))
        dp_o = plan.gather_dp((zj_o.finish()[0], "y"))
        z_d = plan.gather_ctx([wrap(s_d, model_width)])
        found = kv_ring.finish()
        o_t, lse = attend(list(range(len(found))), [kv for _, kv in found], None, True)
    pieces = [piece for _, piece in found]
    d_orders = ("x", "y")[: plan.parts]
    (w_o,) = dp_o.finish()

    o_rel = pick_call(own_at, 1, o_t)
    attn = product_tn((w_o, o_rel))
    inverse_mlp, h2x, h2y, mid = norm_call(own_at, (0, 1), x_t, attn, gain_mlp)
    h2x, h2y, attn = tick((h2x, h2y, attn), dp_u, z_d)
    (d_block,) = z_d.finish()
    dp_d = plan.gather_dp(*zip(plan.row_parts(d_block), d_orders))
    (w_g,) = dp_g.finish()
    (w_u,) = dp_u.finish()
    gate, up, hidden = hidden_call(own_at, abs_at, plan.parts, w_g, w_u, h2x, h2y)
    gate, up, hidden = tick((gate, up, hidden), dp_d, clock=clock)

    x_f = x_t.astype(f32)
    router = jax.nn.sigmoid(jnp.sum(x_f * w_router[:, None], axis=0, keepdims=True))
    bits = gate_mask.astype(f32)
    chosen = bits * router
    usable = (own_pos < seq_length).astype(f32)[None, :]
    dy = cotangent[0].T.astype(f32) * usable
    db = dy * chosen
    d_mlp = db.astype(bf16)
    both_d = []
    for part in hidden:
        both_d.append(plan.halves(part, d_mlp))
        d_mlp, both_d = tick((d_mlp, both_d), dp_d)
    w_d = dp_d.finish()
    r_d = plan.reduce_dp(*[(*both, o) for both, o in zip(both_d, d_orders)])
    mlp = product_tn(*zip(w_d, hidden))
    d_mlp, mlp = tick((d_mlp, mlp), r_d, clock=clock)
    d_gate, d_up = hidden_back_call(own_at, abs_at, gate, up, w_d, d_mlp)
    d_gate, d_up, mlp = tick((d_gate, d_up, mlp), r_d, clock=clock)
    both_g = plan.halves(h2x, d_gate)
    both_u = plan.halves(h2y, d_up)
    d_gate, d_up, both_g, both_u, mlp = tick((d_gate, d_up, both_g, both_u, mlp), r_d)
    r_gu = plan.reduce_dp((*both_g, "x"), (*both_u, "y"))
    dh2x = product_nn(w_g, d_gate)
    dh2y = product_nn(w_u, d_up)
    branch = attn + mlp
    result = (x_f + chosen * branch).astype(bf16).T
    d_logit = bits * jnp.sum(dy * branch, axis=0, keepdims=True) * router * (1.0 - router)
    grad_router = jnp.sum(d_logit * x_f, axis=1)
    dx = dy + d_logit * w_router[:, None]
    dh2x, dh2y, dx, result, grad_router = tick((dh2x, dh2y, dx, result, grad_router), r_gu)
    d_blocks = r_d.finish()
    zr_d = plan.reduce_ctx([jnp.concatenate(d_blocks) if len(d_blocks) > 1 else d_blocks[0]])
    dx, d_attn, grad_gain_mlp = norm_back_call(
        abs_at, [(dh2x, 0), (dh2y, 1)], mid, inverse_mlp, gain_mlp, [(dx, f32), (db, bf16)]
    )
    do_t = pick_call(abs_at, 1, product_nn(w_o, d_attn, bf16))
    both_o = plan.halves(o_rel, d_attn)
    do_t, both_o, dx, grad_gain_mlp = tick((do_t, both_o, dx, grad_gain_mlp), zr_d)
    r_o = plan.reduce_dp((*both_o, "y"))

    def attend_back(offset, dq):
        dq, part = attend_back_call(
            scalars,
            [offsets.index(offset)],
            q_t,
            do_t,
            o_t,
            lse,
            [pieces[offsets.index(offset)]],
            dq,
            [bf16 if offset else f32],
            group_size,
            head_width,
        )
        return dq, part

    def turn_back(d_kv):
        dk_t = rotate_t(d_kv[0], cosine, -sine, head_width).astype(bf16)
        return dk_t, d_kv[1].astype(bf16)

    dq = None
    if by_rows and ctx_size == 4:
        dq, far = attend_back(-2, None)
        dq, far, do_t, dx = tick((dq, far, do_t, dx), zr_d, r_o, clock=clock)
        far_moving = shift_ctx(far, -1).launch(far)
        dq, back = attend_back(-1, dq)
        dq, back, far_moving, do_t = tick((dq, back, far_moving, do_t), r_gu, clock=clock)
        back = (back.astype(f32) + far_moving.astype(f32)).astype(bf16)
        back_moving = shift_ctx(back, -1).launch(back)
        dq, ahead = attend_back(1, dq)
        dq, ahead, back_moving, do_t = tick(
            (dq, ahead, back_moving, do_t), r_o, clock=clock
        )
        ahead_moving = shift_ctx(ahead, 1).launch(ahead)
        dq, own = attend_back(0, dq)
        dq, own, ahead_moving = tick((dq, own, ahead_moving), r_gu, r_o)
        dq_t = rotate_t(dq * head_width**-0.5, cosine, -sine, head_width).astype(bf16)
        both_q = plan.halves(h1x, dq_t)
        zr_mlp = plan.reduce_ctx(r_gu.finish() + r_o.finish())
        d_kv = own.astype(f32) + back_moving.astype(f32) + ahead_moving.astype(f32)
    else:
        parts = {}
        for offset in sorted(offsets, key=lambda o: -abs(o)):
            dq, parts[offset] = attend_back(offset, dq)
        d_kv = Job(reduce_ring_steps(parts)).finish()
        dq_t = rotate_t(dq * head_width**-0.5, cosine, -sine, head_width).astype(bf16)
        both_q = plan.halves(h1x, dq_t)
        zr_mlp = plan.reduce_ctx(r_gu.finish() + r_o.finish())
    dk_t, dv_t = turn_back(d_kv)
    dkv_t = jnp.concatenate([dk_t, dv_t])
    both_kv = plan.halves(h1y, dkv_t)
    r_qkv = plan.reduce_dp((*both_kv, "y"), (*both_q, "x"))
    dh1x = product_nn(w_q, dq_t)
    dh1y = product_nn(w_kv, dkv_t)
    dh1x, dh1y = tick((dh1x, dh1y), r_qkv)
    grad_tokens, grad_gain_attn = norm_back_call(
        abs_at, [(dh1x, 0), (dh1y, 1)], x_t, inverse_attn, gain_attn, [(dx, bf16)]
    )
    small_job = plan.sum_all(jnp.stack([grad_gain_attn, grad_gain_mlp, grad_router]))
    (grad_tokens,) = tick((grad_tokens,), r_qkv, zr_mlp, small_job)
    grad_tokens = grad_tokens.T
    (grad_tokens,) = tick((grad_tokens,), r_qkv, small_job)
    kv_sum, q_sum = r_qkv.finish()
    zr_qkv = plan.reduce_ctx([kv_sum[:, :kv_width], kv_sum[:, kv_width:], q_sum])
    (grad_tokens,) = tick((grad_tokens,), zr_qkv, zr_mlp, small_job)
    (grad_down,) = zr_d.finish()
    grad_gate, grad_up, grad_out = zr_mlp.finish()
    grad_tokens, grad_down, grad_gate, grad_up, grad_out = tick(
        (grad_tokens, grad_down, grad_gate, grad_up, grad_out), zr_qkv, small_job
    )
    grad_key, grad_value, grad_query = zr_qkv.finish()
    small = small_job.finish()
    return (
        result[None],
        grad_tokens[None],
        grad_query,
        grad_key,
        grad_value,
        grad_out,
        grad_gate,
        grad_up,
        grad_down,
        small[0],
        small[1],
        small[2],
    )


def solution(mesh):
    rows = P("dp", "ctx", None)
    flat = P(("dp", "ctx"))
    return jax.shard_map(
        per_device,
        mesh=mesh,
        in_specs=(rows, rows, P("dp"), P("dp", "ctx"), P()) + (flat,) * 7 + (P(),) * 3,
        out_specs=(rows, rows) + (flat,) * 7 + (P(),) * 3,
        check_vma=False,
    )
```
